32 devices in a mesh: src: 4 (over y, core), tgt: 8 (over z, x).
Axes of the slice: x: 2, y: 2, z: 4, core: 2. Of those that a mesh axis runs over, the one named last changes fastest.
Arguments:
- kernel: bfloat16 [32768, 8192], P('tgt', 'src'), may hold values from -6 to 6
- probes: bfloat16 [3, 64, 8192], P(None, None, 'src'), may hold values from -6 to 6
Outputs:
- middle_basis: float32 [4, 64, 32768], P('src', None, 'tgt')
- coarse_basis: float32 [4, 64, 8, 4096], P(None, None, 'tgt', 'src')
The draws below stay inside these ranges and needn't reach their ends.
All inputs are finite; a program needn't handle non-finite values.
Results may differ from the reference program's by a relative error of at most 0.0003.
Values sent between devices are 32-bit elements; how exact they have to be, the bound alone decides.
A program may use at most 64 MiB of HBM per device.

```python
import math
import jax
import jax.numpy as jnp
from jax import lax

R = 64
ROWS = 4096
COLS = 2048
TROWS = 32768
SCOLS = 8192
N_SRC = 4
N_TGT = 8


def shard_levels(own_key, shape, split, least, top_value):
    def one(position, parts):
        heights = jax.random.uniform(jax.random.fold_in(jax.random.fold_in(own_key, 6), position), (parts,), jnp.float32, least / len(split), top_value / len(split))
        return jnp.repeat(jnp.exp(heights), shape[position] // parts).reshape((-1,) + (1,) * (len(shape) - position - 1))

    loudness = one(*split[0])
    for cut in split[1:]:
        loudness = loudness * one(*cut)
    return loudness


def centred(key, extent, spread, bound, pieces=(), held_as=jnp.bfloat16):
    values = jax.random.normal(key, extent, jnp.float32) * spread
    if len(pieces) > 0:
        values = shard_levels(key, extent, pieces, -0.22, 0.18) * values
    return jnp.clip(values, min=-bound, max=bound).astype(held_as)


def setup_inputs(seed: int = 0) -> dict:
    seeds = jax.random.split(jax.random.key(seed), 3)
    return {
        "kernel": centred(seeds[0], (TROWS, SCOLS), 1.0, 6.0, ((0, 8), (1, 4))),
        "probes": centred(seeds[1], (3, R, SCOLS), 1.0, 6.0, ((2, 4),)),
    }


highest = lax.Precision.HIGHEST

def cross_products(left, right):
    return jnp.einsum('...rm,...sm->...rs', left, right, precision=highest)

def combine_rows(weights, basis):
    return jnp.einsum('...rs,...sm->...rm', weights, basis, precision=highest)

def orthonormal(values, gram):
    factor = jnp.linalg.cholesky(gram)
    return jax.scipy.linalg.solve_triangular(factor, values, lower=True)

def complement(values, basis):
    coefficient = cross_products(values, basis)
    remainder = values - combine_rows(coefficient, basis)
    return orthonormal(remainder, cross_products(remainder, remainder))

def reference(kernel, probes):
    blocks = jnp.arange(N_SRC, dtype=jnp.int32)

    def sketch(level):

        def one_block(index):
            start = (index * COLS).astype(jnp.int32)
            columns = lax.dynamic_slice_in_dim(kernel, start, COLS, 1)
            probe = lax.dynamic_slice_in_dim(probes[level], start, COLS, 1)
            return lax.dot_general(probe.astype(jnp.float32), columns.astype(jnp.float32), (((1,), (1,)), ((), ())), preferred_element_type=jnp.float32)
        return lax.map(one_block, blocks)
    first = sketch(0)
    fine = orthonormal(first, cross_products(first, first))
    second = sketch(1)
    paired = second.reshape(N_SRC // 2, 2, R, TROWS).sum(axis=1)
    pair_sum = jnp.repeat(paired, 2, axis=0)
    middle = complement(pair_sum, fine)
    third = sketch(2)
    grouped = third.reshape(N_SRC // 4, 4, R, TROWS).sum(axis=1)
    group_sum = jnp.repeat(grouped, 4, axis=0)
    coarse = complement(group_sum, jnp.concatenate((fine, middle), axis=1))
    scale = math.sqrt(TROWS)
    return (middle * scale, (coarse * scale).reshape(N_SRC, R, N_TGT, ROWS))
```

```python
import functools
import math

import jax
import jax.numpy as jnp
from jax import lax
from jax.experimental import pallas as pl
from jax.experimental.pallas import tpu as pltpu
from jax.sharding import PartitionSpec as P

highest = lax.Precision.HIGHEST
MESH = pl.DeviceIdType.MESH


def nt_dot(a, b):
    return lax.dot_general(a, b, (((1,), (1,)), ((), ())), preferred_element_type=jnp.float32)


def split(value):
    high = value.astype(jnp.bfloat16)
    return high, (value - high.astype(jnp.float32)).astype(jnp.bfloat16)


def inverse_factor(a, chunk=16):
    n = a.shape[0]
    lanes = 2 * n
    m = jnp.concatenate([a, jnp.eye(n, dtype=a.dtype)], axis=1)
    blocks = [m[8 * r:8 * r + 8] for r in range(n // 8)]
    row_ids = lax.broadcasted_iota(jnp.int32, (8, lanes), 0)
    for start in range(0, n, chunk):
        cols = [{r: jnp.broadcast_to(blocks[r][:, start + q:start + q + 1], (8, lanes))
                 for r in range(start // 8, n // 8)} for q in range(chunk)]
        for q in range(chunk):
            top, inner = divmod(start + q, 8)
            inv = 1.0 / jnp.broadcast_to(cols[q][top][inner:inner + 1], (8, lanes))
            row = jnp.broadcast_to(blocks[top][inner:inner + 1], (8, lanes)) * inv
            later = {p: jnp.broadcast_to(cols[p][top][inner:inner + 1], (8, lanes)) * inv for p in range(q + 1, chunk)}
            for r in range(top, n // 8):
                mult = cols[q][r]
                if r == top:
                    mult = jnp.where(row_ids > inner, mult, 0.0)
                for p in later:
                    cols[p][r] = cols[p][r] - mult * later[p]
                blocks[r] = blocks[r] - mult * row
    m = jnp.concatenate(blocks, axis=0)
    r_ids = lax.broadcasted_iota(jnp.int32, (n, lanes), 0)
    c_ids = lax.broadcasted_iota(jnp.int32, (n, lanes), 1)
    pivots = jnp.sum(jnp.where(r_ids == c_ids, m, 0.0), axis=1, keepdims=True)
    return m[:, n:] * (1.0 / jnp.sqrt(pivots))


def mm(a, b):
    return lax.dot_general(a, b, (((1,), (0,)), ((), ())), precision=highest, preferred_element_type=jnp.float32)


def mmt(a, b):
    return lax.dot_general(a, b, (((1,), (1,)), ((), ())), precision=highest, preferred_element_type=jnp.float32)


def flip(index, mask):
    result = 0
    place = 1
    while place <= mask:
        bit = lax.rem(index // place, 2)
        result = result + place * ((1 - bit) if mask & place else bit)
        place *= 2
    return result + (index // place) * place


def remote(src, dst, send, recv, device):
    return pltpu.make_async_remote_copy(
        src_ref=src, dst_ref=dst, send_sem=send, recv_sem=recv, device_id=device, device_id_type=MESH)


class Reduction:
    def __init__(self, n, parts, pieces, summed, full, sems):
        self.n, self.parts, self.pieces, self.summed, self.full = n, parts, pieces, summed, full
        self.r_send, self.r_recv, self.g_send, self.g_recv = (sems.at[k] for k in range(4))
        self.t = lax.axis_index("tgt")

    def scatter(self, value):
        rows = value.shape[0] // self.n
        for p in range(self.n):
            self.parts[p] = value[p * rows:(p + 1) * rows]
        self.sent = []
        for d in range(1, self.n):
            to = lax.rem(self.t + d, self.n)
            self.sent.append(remote(self.parts.at[to], self.pieces.at[d - 1],
                                    self.r_send.at[d - 1], self.r_recv.at[d - 1], {"tgt": to}))
            self.sent[-1].start()

    def gather(self):
        value = self.parts[self.t]
        for d in range(1, self.n):
            self.sent[d - 1].wait_recv()
            value = value + self.pieces[d - 1]
        self.summed[...] = value
        self.full[self.t] = value
        for d in range(1, self.n):
            to = lax.rem(self.t + d, self.n)
            self.sent.append(remote(self.summed, self.full.at[self.t],
                                    self.g_send.at[d - 1], self.g_recv.at[d - 1], {"tgt": to}))
            self.sent[-1].start()

    def result(self):
        for d in range(1, self.n):
            origin = lax.rem(self.t + self.n - d, self.n)
            remote(self.summed, self.full.at[origin], self.g_send.at[d - 1], self.g_recv.at[d - 1],
                   {"tgt": origin}).wait_recv()
        return jnp.concatenate([self.full[p] for p in range(self.n)], axis=0)

    def drain(self):
        for copy in self.sent:
            copy.wait_send()


def moved_rows(mask, rank):
    return rank * (3 if mask % 4 == 0 else 2 if mask % 2 == 0 else 1)


def product(weights, operand):
    w_high, w_low = weights
    high, low = operand
    count = w_high.shape[0]
    both = jnp.dot(jnp.concatenate([w_high, w_low], axis=0), high, preferred_element_type=jnp.float32)
    return both[:count] + (both[count:] + jnp.dot(w_high, low, preferred_element_type=jnp.float32))


def bases_kernel(n_src, n_tgt, tiles, tile, slots, before, rank, scale,
                 kernel_hbm, probes_hbm, middle_ref, coarse_ref,
                 held, probes_ref, own, shared, stack, chip, total, moved, weights,
                 parts_a, pieces_a, summed_a, full_a, parts_b, pieces_b, summed_b, full_b,
                 k_sem, p_sem, a_send, a_recv, b_send, b_recv, c_send, c_recv,
                 ra_sems, rb_sems, m_send, m_recv, w_send, w_recv, hops):
    s = lax.axis_index("src")
    t = lax.axis_index("tgt")
    core = lax.rem(s, 2)
    mate = flip(s, 1)
    across = flip(s, 2)
    half = rank // 2
    per = tiles // n_src

    barrier = pltpu.get_barrier_semaphore()
    for mask in range(1, n_src):
        pl.semaphore_signal(barrier, inc=1, device_id={"src": flip(s, mask)}, device_id_type=MESH)
    ring = ((t + 1 - 2 * lax.rem(t, 2), t >= 0), (t - 2, t >= 2), (t + 2, t + 2 < n_tgt))
    degree = 1 + jnp.where(t >= 2, 1, 0) + jnp.where(t + 2 < n_tgt, 1, 0)

    def greet(semaphore):
        for to, exists in ring:
            @pl.when(exists)
            def _(to=to):
                pl.semaphore_signal(semaphore, inc=1, device_id={"tgt": to}, device_id_type=MESH)

    greet(barrier)

    def fetch(i):
        slot = lax.rem(i, slots)
        return pltpu.make_async_copy(
            kernel_hbm.at[pl.ds(pl.multiple_of(i * tile, tile), tile)], held.at[slot], k_sem.at[slot])

    fetch_probes = pltpu.make_async_copy(probes_hbm, probes_ref, p_sem)
    fetch_probes.start()
    for i in range(min(slots, tiles)):
        fetch(i).start()

    mine = pl.multiple_of(half * core, half)
    theirs = pl.multiple_of(half * (1 - core), half)

    def share_pair(j):
        return remote(own.at[j, pl.ds(rank, rank)], shared.at[j, pl.ds(0, rank)],
                      a_send.at[0, j], a_recv.at[0, j], {"src": mate})

    def share_group(j):
        return remote(own.at[j, pl.ds(2 * rank + theirs, half)], shared.at[j, pl.ds(rank, half)],
                      a_send.at[1, j], a_recv.at[1, j], {"src": mate})

    def cross_chip(j):
        return remote(chip.at[0, j], chip.at[1, j], b_send.at[j], b_recv.at[j], {"src": across})

    def hand_over(j):
        return remote(chip.at[2, j], stack.at[j, pl.ds(2 * rank + mine, half)],
                      c_send.at[j], c_recv.at[j], {"src": mate})

    def move(mask, q):
        to = flip(s, mask)
        count = moved_rows(mask, rank)
        return remote(stack.at[to * per + q, pl.ds(0, count)], moved.at[mask - 1, q, pl.ds(0, count)],
                      m_send.at[mask - 1, q], m_recv.at[mask - 1, q], {"src": to})

    def tell(mask):
        return remote(weights.at[0], weights.at[mask], w_send.at[mask - 1], w_recv.at[mask - 1],
                      {"src": flip(s, mask)})

    total[...] = jnp.zeros_like(total)

    def compute(i):
        fetch(i).wait()
        own[i] = nt_dot(probes_ref[...], held[lax.rem(i, slots)])

        @pl.when(i + slots < tiles)
        def _():
            fetch(i + slots).start()

    def share(i):
        share_group(i).start()
        share_pair(i).start()

    def send_group(j):
        share_group(j).wait_recv()
        chip[0, j] = own[j, pl.ds(2 * rank + mine, half)] + shared[j, rank:rank + half]
        cross_chip(j).start()

    def lower_gram(j):
        share_pair(j).wait_recv()
        first = own[j, 0:rank]
        second = own[j, rank:2 * rank] + shared[j, 0:rank]
        both = jnp.concatenate([first, second], axis=0)
        stack[j, 0:2 * rank] = both
        high, low = split(both)
        total[...] += nt_dot(high, jnp.concatenate([high, low], axis=0))

    def each(start, stop, *steps):
        def run(i, carry):
            for step in steps:
                step(i)
            return carry
        lax.fori_loop(start, stop, run, 0)

    rounds = n_tgt // 2 - 1

    def spread(r):
        pl.semaphore_wait(hops.at[r], degree)

        @pl.when(r + 1 < rounds)
        def _():
            greet(hops.at[r + 1])

    fetch_probes.wait()
    each(0, before, compute)
    pl.semaphore_wait(barrier, n_src - 1 + degree)
    each(0, before, share)
    greet(hops.at[0])
    compute(before)
    share(before)
    each(0, before, send_group)
    each(0, before, lower_gram)

    def previous(step):
        return lambda i: step(i - 1)

    def spread_at(i):
        r = (i - before - 1) // 2

        @pl.when((lax.rem(i - before - 1, 2) == 0) & (r < rounds))
        def _():
            spread(r)

    each(before + 1, tiles, compute, share, previous(send_group), previous(lower_gram), spread_at)
    send_group(tiles - 1)
    lower_gram(tiles - 1)
    each(min(rounds, (tiles - before) // 2), rounds, spread)

    lower = Reduction(n_tgt, parts_a, pieces_a, summed_a, full_a, ra_sems)
    mixed = total[:, 2 * rank:]
    lower.scatter(total[:, 0:2 * rank] + (mixed + mixed.T))
    late = []
    for mask in (2, 3, 1) + tuple(range(4, n_src)):
        for q in range(per):
            if mask % 4 == 0:
                late.append((mask, q))
            else:
                move(mask, q).start()

    def sum_group(j):
        cross_chip(j).wait_recv()
        value = chip[0, j] + chip[1, j]
        chip[2, j] = value
        stack[j, pl.ds(2 * rank + mine, half)] = value
        hand_over(j).start()

    def upper_gram(j, carry):
        hand_over(j).wait_recv()
        high, low = split(stack[j])
        top = high[2 * rank:]
        return carry + (nt_dot(top, high) + (nt_dot(top, low) + nt_dot(low[2 * rank:], high)))

    def both(j, carry):
        sum_group(j)
        return upper_gram(j - 1, carry)

    sum_group(0)
    early = 5 * tiles // 8
    upper_value = lax.fori_loop(1, early, both, jnp.zeros((rank, 3 * rank), jnp.float32))
    lower.gather()
    upper_value = lax.fori_loop(early, tiles, both, upper_value)
    upper_value = upper_gram(tiles - 1, upper_value)
    for mask, q in late:
        move(mask, q).start()
    upper = Reduction(n_tgt, parts_b, pieces_b, summed_b, full_b, rb_sems)
    upper.scatter(upper_value)

    low_gram = lower.result()
    x0 = inverse_factor(low_gram[0:rank, 0:rank])
    c_pair = mmt(low_gram[rank:, 0:rank], x0)
    rest = low_gram[rank:, rank:] - mmt(c_pair, c_pair)
    x1 = inverse_factor(rest)
    mid_first = -mm(x1, mm(c_pair, x0))
    upper.gather()

    mid_weights = split(jnp.concatenate([scale * mid_first, scale * x1], axis=1))
    for j in range(tiles):
        middle_ref[0, :, j * tile:(j + 1) * tile] = product(mid_weights, split(stack[j, 0:2 * rank]))

    up_gram = upper.result()
    c_first = mmt(up_gram[:, 0:rank], x0)
    c_mid = mmt(up_gram[:, rank:2 * rank] - mmt(c_first, c_pair), x1)
    x2 = inverse_factor(up_gram[:, 2 * rank:] - mmt(c_first, c_first) - mmt(c_mid, c_mid))
    weights[0, :, 0:rank] = -scale * mm(x2, mm(c_first, x0) + mm(c_mid, mid_first))
    weights[0, :, rank:2 * rank] = -scale * mm(x2, mm(c_mid, x1))
    weights[0, :, 2 * rank:] = scale * x2
    for mask in range(1, n_src):
        tell(mask).start()

    lower.drain()
    upper.drain()

    for mask in range(n_src):
        if mask:
            tell(mask).wait_recv()
        its = split(weights[mask])
        for q in range(per):
            if mask:
                move(mask, q).wait_recv()

            def rows(source, index):
                ref = moved.at[source - 1, q] if source else stack.at[s * per + q]
                return ref[index * rank:(index + 1) * rank]

            operand = jnp.concatenate(
                [rows(mask, 0), rows(mask - mask % 2, 1), rows(mask - mask % 4, 2)], axis=0)
            coarse_ref[flip(s, mask), :, 0, q * tile:(q + 1) * tile] = product(its, split(operand))

    def finish(j):
        share_group(j).wait_send()
        share_pair(j).wait_send()
        cross_chip(j).wait_send()
        hand_over(j).wait_send()

    each(0, tiles, finish)
    for mask in range(1, n_src):
        for q in range(per):
            move(mask, q).wait_send()
        tell(mask).wait_send()


def bases(kernel, probes, tile, scale):
    n_src, n_tgt = lax.axis_size("src"), lax.axis_size("tgt")
    rows, cols = kernel.shape
    total_rank = probes.shape[0]
    rank = total_rank // 3
    tiles = rows // tile
    per = tiles // n_src
    slots = min(4, tiles)
    f32 = jnp.float32
    dma = pltpu.SemaphoreType.DMA
    low, up = 2 * rank, rank
    hbm = pl.BlockSpec(memory_space=pltpu.HBM)
    vmem = pl.BlockSpec(memory_space=pltpu.VMEM)
    return pl.pallas_call(
        functools.partial(bases_kernel, n_src, n_tgt, tiles, tile, slots, min(2, tiles - 2), rank, scale),
        out_shape=(jax.ShapeDtypeStruct((1, rank, rows), f32),
                   jax.ShapeDtypeStruct((n_src, rank, 1, per * tile), f32)),
        in_specs=[hbm, hbm],
        out_specs=(vmem, vmem),
        scratch_shapes=[
            pltpu.VMEM((slots, tile, cols), kernel.dtype),
            pltpu.VMEM((total_rank, cols), probes.dtype),
            pltpu.VMEM((tiles, total_rank, tile), f32),
            pltpu.VMEM((tiles, rank + rank // 2, tile), f32),
            pltpu.VMEM((tiles, total_rank, tile), f32),
            pltpu.VMEM((3, tiles, rank // 2, tile), f32),
            pltpu.VMEM((low, 2 * low), f32),
            pltpu.VMEM((n_src - 1, per, total_rank, tile), f32),
            pltpu.VMEM((n_src, rank, total_rank), f32),
            pltpu.VMEM((n_tgt, low // n_tgt, low), f32),
            pltpu.VMEM((n_tgt - 1, low // n_tgt, low), f32),
            pltpu.VMEM((low // n_tgt, low), f32),
            pltpu.VMEM((n_tgt, low // n_tgt, low), f32),
            pltpu.VMEM((n_tgt, up // n_tgt, total_rank), f32),
            pltpu.VMEM((n_tgt - 1, up // n_tgt, total_rank), f32),
            pltpu.VMEM((up // n_tgt, total_rank), f32),
            pltpu.VMEM((n_tgt, up // n_tgt, total_rank), f32),
            dma((slots,)), dma,
            dma((2, tiles)), dma((2, tiles)), dma((tiles,)), dma((tiles,)), dma((tiles,)), dma((tiles,)),
            dma((4, n_tgt - 1)), dma((4, n_tgt - 1)),
            dma((n_src - 1, per)), dma((n_src - 1, per)), dma((n_src - 1,)), dma((n_src - 1,)),
            pltpu.SemaphoreType.REGULAR((max(1, n_tgt // 2 - 1),)),
        ],
        compiler_params=pltpu.CompilerParams(
            collective_id=0, has_side_effects=True, vmem_limit_bytes=48 * 2 ** 20),
        name="bases",
    )(kernel, probes)


def store_kernel(middle_in, coarse_in, middle_ref, coarse_ref, sems):
    copies = [pltpu.make_async_copy(middle_in, middle_ref, sems.at[0]),
              pltpu.make_async_copy(coarse_in, coarse_ref, sems.at[1])]
    for copy in copies:
        copy.start()
    for copy in copies:
        copy.wait()


def store(middle, coarse):
    anywhere = pl.BlockSpec(memory_space=pl.ANY)
    return pl.pallas_call(
        store_kernel,
        out_shape=tuple(jax.ShapeDtypeStruct(x.shape, x.dtype) for x in (middle, coarse)),
        in_specs=[anywhere, anywhere],
        out_specs=(anywhere, anywhere),
        scratch_shapes=[pltpu.SemaphoreType.DMA((2,))],
        compiler_params=pltpu.CompilerParams(vmem_limit_bytes=2 ** 20),
        name="store",
    )(middle, coarse)


def shards(kernel, probes):
    n_src, n_tgt = lax.axis_size("src"), lax.axis_size("tgt")
    rows = kernel.shape[0]
    scale = math.sqrt(rows * n_tgt)
    levels, rank, cols = probes.shape
    tile = min(512, rows // n_src)
    return store(*bases(kernel, probes.reshape(levels * rank, cols), tile, scale))


def solution(mesh):
    placed = (P("tgt", "src"), P(None, None, "src"))
    return jax.shard_map(
        shards,
        mesh=mesh,
        in_specs=placed,
        out_specs=(P("src", None, "tgt"), P(None, None, "tgt", "src")),
        check_vma=False,
    )
```

```python
import functools
import math

import jax
import jax.numpy as jnp
from jax import lax
from jax.experimental import pallas as pl
from jax.experimental.pallas import tpu as pltpu
from jax.sharding import PartitionSpec as P

highest = lax.Precision.HIGHEST
MESH = pl.DeviceIdType.MESH


def nt_dot(a, b):
    return lax.dot_general(a, b, (((1,), (1,)), ((), ())), preferred_element_type=jnp.float32)


def split(value):
    high = value.astype(jnp.bfloat16)
    return high, (value - high.astype(jnp.float32)).astype(jnp.bfloat16)


def inverse_factor(a, chunk=16):
    n = a.shape[0]
    lanes = 2 * n
    m = jnp.concatenate([a, jnp.eye(n, dtype=a.dtype)], axis=1)
    blocks = [m[8 * r:8 * r + 8] for r in range(n // 8)]
    row_ids = lax.broadcasted_iota(jnp.int32, (8, lanes), 0)
    for start in range(0, n, chunk):
        cols = [{r: jnp.broadcast_to(blocks[r][:, start + q:start + q + 1], (8, lanes))
                 for r in range(start // 8, n // 8)} for q in range(chunk)]
        for q in range(chunk):
            top, inner = divmod(start + q, 8)
            inv = 1.0 / jnp.broadcast_to(cols[q][top][inner:inner + 1], (8, lanes))
            row = jnp.broadcast_to(blocks[top][inner:inner + 1], (8, lanes)) * inv
            later = {p: jnp.broadcast_to(cols[p][top][inner:inner + 1], (8, lanes)) * inv for p in range(q + 1, chunk)}
            for r in range(top, n // 8):
                mult = cols[q][r]
                if r == top:
                    mult = jnp.where(row_ids > inner, mult, 0.0)
                for p in later:
                    cols[p][r] = cols[p][r] - mult * later[p]
                blocks[r] = blocks[r] - mult * row
    m = jnp.concatenate(blocks, axis=0)
    r_ids = lax.broadcasted_iota(jnp.int32, (n, lanes), 0)
    c_ids = lax.broadcasted_iota(jnp.int32, (n, lanes), 1)
    pivots = jnp.sum(jnp.where(r_ids == c_ids, m, 0.0), axis=1, keepdims=True)
    return m[:, n:] * (1.0 / jnp.sqrt(pivots))


def mm(a, b):
    return lax.dot_general(a, b, (((1,), (0,)), ((), ())), precision=highest, preferred_element_type=jnp.float32)


def mmt(a, b):
    return lax.dot_general(a, b, (((1,), (1,)), ((), ())), precision=highest, preferred_element_type=jnp.float32)


def flip(index, mask):
    result = 0
    place = 1
    while place <= mask:
        bit = lax.rem(index // place, 2)
        result = result + place * ((1 - bit) if mask & place else bit)
        place *= 2
    return result + (index // place) * place


def remote(src, dst, send, recv, device):
    return pltpu.make_async_remote_copy(
        src_ref=src, dst_ref=dst, send_sem=send, recv_sem=recv, device_id=device, device_id_type=MESH)


class Reduction:
    def __init__(self, n, parts, pieces, summed, full, sems):
        self.n, self.parts, self.pieces, self.summed, self.full = n, parts, pieces, summed, full
        self.r_send, self.r_recv, self.g_send, self.g_recv = (sems.at[k] for k in range(4))
        self.t = lax.axis_index("tgt")

    def piece(self, d):
        to = lax.rem(self.t + d, self.n)
        return remote(self.parts.at[to], self.pieces.at[d - 1], self.r_send.at[d - 1], self.r_recv.at[d - 1], {"tgt": to})

    def share(self, d):
        to = lax.rem(self.t + d, self.n)
        return remote(self.summed, self.full.at[self.t], self.g_send.at[d - 1], self.g_recv.at[d - 1], {"tgt": to})

    def scatter(self, value):
        rows = value.shape[0] // self.n
        for p in range(self.n):
            self.parts[p] = value[p * rows:(p + 1) * rows]
        for d in range(1, self.n):
            self.piece(d).start()

    def gather(self):
        value = self.parts[self.t]
        for d in range(1, self.n):
            self.piece(d).wait_recv()
            value = value + self.pieces[d - 1]
        self.summed[...] = value
        self.full[self.t] = value
        for d in range(1, self.n):
            self.share(d).start()

    def result(self):
        for d in range(1, self.n):
            origin = lax.rem(self.t + self.n - d, self.n)
            remote(self.summed, self.full.at[origin], self.g_send.at[d - 1], self.g_recv.at[d - 1],
                   {"tgt": origin}).wait_recv()
        return jnp.concatenate([self.full[p] for p in range(self.n)], axis=0)

    def drain(self):
        for d in range(1, self.n):
            self.piece(d).wait_send()
            self.share(d).wait_send()


def moved_rows(mask, rank):
    return rank * (3 if mask % 4 == 0 else 2 if mask % 2 == 0 else 1)


def product(weights, operand):
    w_high, w_low = weights
    high, low = operand
    count = w_high.shape[0]
    both = jnp.dot(jnp.concatenate([w_high, w_low], axis=0), high, preferred_element_type=jnp.float32)
    return both[:count] + (both[count:] + jnp.dot(w_high, low, preferred_element_type=jnp.float32))


def bases_kernel(n_src, n_tgt, tiles, tile, slots, before, rank, scale,
                 kernel_hbm, probes_hbm, middle_ref, coarse_ref,
                 held, probes_ref, own, shared, stack, chip, total, moved, weights,
                 parts_a, pieces_a, summed_a, full_a, parts_b, pieces_b, summed_b, full_b,
                 k_sem, p_sem, a_send, a_recv, b_send, b_recv, c_send, c_recv,
                 ra_sems, rb_sems, m_send, m_recv, w_send, w_recv, hops, h_send, h_recv,
                 pivots, factors, low, pair_first, basis, fit):
    s = lax.axis_index("src")
    t = lax.axis_index("tgt")
    core = lax.rem(s, 2)
    mate = flip(s, 1)
    across = flip(s, 2)
    half = rank // 2
    per = tiles // n_src
    first_tile = (across - lax.rem(across, 2)) * per
    first_sum = (s - lax.rem(s, 2)) * per

    def at(i):
        return lax.rem(i + first_tile, tiles)

    def sum_at(i):
        return lax.rem(i + first_sum, tiles)


    barrier = pltpu.get_barrier_semaphore()
    for mask in range(1, n_src):
        pl.semaphore_signal(barrier, inc=1, device_id={"src": flip(s, mask)}, device_id_type=MESH)
    ring = ((t + 1 - 2 * lax.rem(t, 2), t >= 0), (t - 2, t >= 2), (t + 2, t + 2 < n_tgt))
    degree = 1 + jnp.where(t >= 2, 1, 0) + jnp.where(t + 2 < n_tgt, 1, 0)

    def greet(semaphore):
        for to, exists in ring:
            @pl.when(exists)
            def _(to=to):
                pl.semaphore_signal(semaphore, inc=1, device_id={"tgt": to}, device_id_type=MESH)

    greet(barrier)

    def fetch(i):
        slot = lax.rem(i, slots)
        return pltpu.make_async_copy(
            kernel_hbm.at[pl.ds(pl.multiple_of(at(i) * tile, tile), tile)], held.at[slot], k_sem.at[slot])

    fetch_probes = pltpu.make_async_copy(probes_hbm, probes_ref, p_sem)
    fetch_probes.start()
    for i in range(min(slots, tiles)):
        fetch(i).start()

    mine = pl.multiple_of(half * core, half)
    theirs = pl.multiple_of(half * (1 - core), half)

    def share_pair(j):
        return remote(own.at[j, pl.ds(rank, rank)], shared.at[j, pl.ds(0, rank)],
                      a_send.at[0, j], a_recv.at[0, j], {"src": mate})

    def share_group(j):
        return remote(own.at[j, pl.ds(2 * rank + theirs, half)], shared.at[j, pl.ds(rank, half)],
                      a_send.at[1, j], a_recv.at[1, j], {"src": mate})

    def cross_chip(j):
        return remote(chip.at[0, j], chip.at[1, j], b_send.at[j], b_recv.at[j], {"src": across})

    def hand_over(j):
        return remote(chip.at[2, j], stack.at[j, pl.ds(2 * rank + mine, half)],
                      c_send.at[j], c_recv.at[j], {"src": mate})

    def move(mask, q):
        to = flip(s, mask)
        count = moved_rows(mask, rank)
        skip = half if (mask in (2, 3) and q == 0) else 0
        rows = pl.ds(skip, count - skip)
        return remote(stack.at[to * per + q, rows], moved.at[mask - 1, q, rows],
                      m_send.at[mask - 1, q], m_recv.at[mask - 1, q], {"src": to})

    def head(mask):
        to = flip(s, mask)
        return remote(own.at[to * per, pl.ds(0, half)], moved.at[mask - 1, 0, pl.ds(0, half)],
                      h_send.at[mask - 2], h_recv.at[mask - 2], {"src": to})

    def heads(even):
        for mask in (2, 3):
            @pl.when((lax.rem(flip(s, mask), 2) == 0) == even)
            def _(mask=mask):
                head(mask).start()

    def tell(mask):
        return remote(weights.at[0], weights.at[mask], w_send.at[mask - 1], w_recv.at[mask - 1],
                      {"src": flip(s, mask)})

    total[...] = jnp.zeros_like(total)

    def compute(i):
        fetch(i).wait()
        own[at(i)] = nt_dot(probes_ref[...], held[lax.rem(i, slots)])

        @pl.when(i + slots < tiles)
        def _():
            fetch(i + slots).start()

    def share(i):
        share_group(at(i)).start()
        share_pair(at(i)).start()

    def send_group(i):
        j = at(i)
        share_group(j).wait_recv()
        chip[0, j] = own[j, pl.ds(2 * rank + mine, half)] + shared[j, rank:rank + half]
        cross_chip(j).start()

    def lower_gram(j):
        share_pair(j).wait_recv()
        first = own[j, 0:rank]
        second = own[j, rank:2 * rank] + shared[j, 0:rank]
        both = jnp.concatenate([first, second], axis=0)
        stack[j, 0:2 * rank] = both
        high, low = split(both)
        total[...] += nt_dot(high, jnp.concatenate([high, low], axis=0))

    def each(start, stop, *steps):
        def run(i, carry):
            for step in steps:
                step(i)
            return carry
        lax.fori_loop(start, stop, run, 0)

    rounds = n_tgt // 2 - 1

    def spread(r):
        pl.semaphore_wait(hops.at[r], degree)

        @pl.when(r + 1 < rounds)
        def _():
            greet(hops.at[r + 1])

    fetch_probes.wait()
    each(0, before, compute)
    pl.semaphore_wait(barrier, n_src - 1 + degree)
    heads(True)
    each(0, before, share)
    greet(hops.at[0])
    compute(before)
    share(before)
    each(0, before, send_group)

    def previous(step):
        return lambda i: step(i - 1)

    def spread_at(i):
        r = (i - before - 1) // 2

        @pl.when((lax.rem(i - before - 1, 2) == 0) & (r < rounds))
        def _():
            spread(r)

    each(before + 1, tiles, compute, share, previous(send_group), spread_at)
    send_group(tiles - 1)
    each(0, tiles, lower_gram)
    each(min(rounds, (tiles - before) // 2), rounds, spread)

    lower = Reduction(n_tgt, parts_a, pieces_a, summed_a, full_a, ra_sems)
    mixed = total[:, 2 * rank:]
    lower.scatter(total[:, 0:2 * rank] + (mixed + mixed.T))
    heads(False)
    late = []
    for mask in (2, 3, 1) + tuple(range(4, n_src)):
        for q in range(per):
            if mask % 4 == 0:
                late.append((mask, q))
            else:
                move(mask, q).start()

    def sum_group(i):
        j = sum_at(i)
        cross_chip(j).wait_recv()
        value = chip[0, j] + chip[1, j]
        chip[2, j] = value
        stack[j, pl.ds(2 * rank + mine, half)] = value
        hand_over(j).start()

    def upper_gram(i, carry):
        j = sum_at(i)
        hand_over(j).wait_recv()
        high, low = split(stack[j])
        top = high[2 * rank:]
        return carry + (nt_dot(top, high) + (nt_dot(top, low) + nt_dot(low[2 * rank:], high)))

    def both(j, carry):
        sum_group(j)
        return upper_gram(j - 1, carry)

    upper = Reduction(n_tgt, parts_b, pieces_b, summed_b, full_b, rb_sems)
    rows_of = lax.broadcasted_iota(jnp.int32, (rank, rank), 0)
    pivots[...] = jnp.where(rows_of == lax.broadcasted_iota(jnp.int32, (rank, rank), 1), 1.0, 0.0)

    def stage(k, carry):
        @pl.when(k == 1)
        def _():
            early = 5 * tiles // 8
            each(0, early, sum_group)
            upper_value = lax.fori_loop(0, early - 1, upper_gram, jnp.zeros((rank, 3 * rank), jnp.float32))
            lower.gather()
            upper_value = lax.fori_loop(early, tiles, both, upper_value)
            upper_value = upper_gram(tiles - 1, upper_value)
            for mask, q in late:
                move(mask, q).start()
            upper.scatter(upper_value)
            low[...] = lower.result()
            pivots[...] = low[0:rank, 0:rank]

        @pl.when(k == 2)
        def _():
            first = factors[1]
            c_pair = mmt(low[rank:, 0:rank], first)
            pivots[...] = low[rank:, rank:] - mmt(c_pair, c_pair)
            pair_first[...] = mm(c_pair, first)
            upper.gather()

        @pl.when(k == 3)
        def _():
            first, second = factors[1], factors[2]
            basis[...] = jnp.concatenate(
                [jnp.concatenate([first, jnp.zeros_like(first)], axis=1),
                 jnp.concatenate([-mm(second, pair_first[...]), second], axis=1)], axis=0)
            up_gram = upper.result()
            coef = mmt(up_gram[:, 0:2 * rank], basis[...])
            pivots[...] = up_gram[:, 2 * rank:] - mmt(coef, coef)
            fit[...] = mm(coef, basis[...])

        factors[k] = inverse_factor(pivots[...])
        return carry

    lax.fori_loop(0, 4, stage, 0)
    x2 = factors[3]
    weights[0, :, 0:2 * rank] = -scale * mm(x2, fit[...])
    weights[0, :, 2 * rank:] = scale * x2
    for mask in range(1, n_src):
        tell(mask).start()

    mid_weights = split(scale * basis[rank:])
    for j in range(tiles):
        middle_ref[0, :, j * tile:(j + 1) * tile] = product(mid_weights, split(stack[j, 0:2 * rank]))

    lower.drain()
    upper.drain()

    for mask in range(n_src):
        if mask:
            tell(mask).wait_recv()
        its = split(weights[mask])
        for q in range(per):
            if mask:
                move(mask, q).wait_recv()
                if mask in (2, 3) and q == 0:
                    head(mask).wait_recv()

            def rows(source, index):
                ref = moved.at[source - 1, q] if source else stack.at[s * per + q]
                return ref[index * rank:(index + 1) * rank]

            operand = jnp.concatenate(
                [rows(mask, 0), rows(mask - mask % 2, 1), rows(mask - mask % 4, 2)], axis=0)
            coarse_ref[flip(s, mask), :, 0, q * tile:(q + 1) * tile] = product(its, split(operand))

    def finish(j):
        share_group(j).wait_send()
        share_pair(j).wait_send()
        cross_chip(j).wait_send()
        hand_over(j).wait_send()

    each(0, tiles, finish)
    for mask in range(1, n_src):
        for q in range(per):
            move(mask, q).wait_send()
        tell(mask).wait_send()
    for mask in (2, 3):
        head(mask).wait_send()


def bases(kernel, probes, tile, scale):
    n_src, n_tgt = lax.axis_size("src"), lax.axis_size("tgt")
    rows, cols = kernel.shape
    total_rank = probes.shape[0]
    rank = total_rank // 3
    tiles = rows // tile
    per = tiles // n_src
    slots = min(4, tiles)
    f32 = jnp.float32
    dma = pltpu.SemaphoreType.DMA
    low, up = 2 * rank, rank
    hbm = pl.BlockSpec(memory_space=pltpu.HBM)
    vmem = pl.BlockSpec(memory_space=pltpu.VMEM)
    return pl.pallas_call(
        functools.partial(bases_kernel, n_src, n_tgt, tiles, tile, slots, min(2, tiles - 2), rank, scale),
        out_shape=(jax.ShapeDtypeStruct((1, rank, rows), f32),
                   jax.ShapeDtypeStruct((n_src, rank, 1, per * tile), f32)),
        in_specs=[hbm, hbm],
        out_specs=(vmem, vmem),
        scratch_shapes=[
            pltpu.VMEM((slots, tile, cols), kernel.dtype),
            pltpu.VMEM((total_rank, cols), probes.dtype),
            pltpu.VMEM((tiles, total_rank, tile), f32),
            pltpu.VMEM((tiles, rank + rank // 2, tile), f32),
            pltpu.VMEM((tiles, total_rank, tile), f32),
            pltpu.VMEM((3, tiles, rank // 2, tile), f32),
            pltpu.VMEM((low, 2 * low), f32),
            pltpu.VMEM((n_src - 1, per, total_rank, tile), f32),
            pltpu.VMEM((n_src, rank, total_rank), f32),
            pltpu.VMEM((n_tgt, low // n_tgt, low), f32),
            pltpu.VMEM((n_tgt - 1, low // n_tgt, low), f32),
            pltpu.VMEM((low // n_tgt, low), f32),
            pltpu.VMEM((n_tgt, low // n_tgt, low), f32),
            pltpu.VMEM((n_tgt, up // n_tgt, total_rank), f32),
            pltpu.VMEM((n_tgt - 1, up // n_tgt, total_rank), f32),
            pltpu.VMEM((up // n_tgt, total_rank), f32),
            pltpu.VMEM((n_tgt, up // n_tgt, total_rank), f32),
            dma((slots,)), dma,
            dma((2, tiles)), dma((2, tiles)), dma((tiles,)), dma((tiles,)), dma((tiles,)), dma((tiles,)),
            dma((4, n_tgt - 1)), dma((4, n_tgt - 1)),
            dma((n_src - 1, per)), dma((n_src - 1, per)), dma((n_src - 1,)), dma((n_src - 1,)),
            pltpu.SemaphoreType.REGULAR((max(1, n_tgt // 2 - 1),)), dma((2,)), dma((2,)),
            pltpu.VMEM((rank, rank), f32), pltpu.VMEM((4, rank, rank), f32), pltpu.VMEM((low, low), f32),
            pltpu.VMEM((rank, rank), f32), pltpu.VMEM((low, low), f32), pltpu.VMEM((rank, low), f32),
        ],
        compiler_params=pltpu.CompilerParams(
            collective_id=0, has_side_effects=True, vmem_limit_bytes=48 * 2 ** 20),
        name="bases",
    )(kernel, pltpu.with_memory_space_constraint(probes, pltpu.HBM))


def store_kernel(middle_in, coarse_in, middle_ref, coarse_ref, sems):
    copies = [pltpu.make_async_copy(middle_in, middle_ref, sems.at[0]),
              pltpu.make_async_copy(coarse_in, coarse_ref, sems.at[1])]
    for copy in copies:
        copy.start()
    for copy in copies:
        copy.wait()


def store(middle, coarse):
    anywhere = pl.BlockSpec(memory_space=pl.ANY)
    return pl.pallas_call(
        store_kernel,
        out_shape=tuple(jax.ShapeDtypeStruct(x.shape, x.dtype) for x in (middle, coarse)),
        in_specs=[anywhere, anywhere],
        out_specs=(anywhere, anywhere),
        scratch_shapes=[pltpu.SemaphoreType.DMA((2,))],
        compiler_params=pltpu.CompilerParams(vmem_limit_bytes=2 ** 20),
        name="store",
    )(middle, coarse)


def shards(kernel, probes):
    n_src, n_tgt = lax.axis_size("src"), lax.axis_size("tgt")
    rows = kernel.shape[0]
    scale = math.sqrt(rows * n_tgt)
    levels, rank, cols = probes.shape
    tile = min(512, rows // n_src)
    return store(*bases(kernel, probes.reshape(levels * rank, cols), tile, scale))


def solution(mesh):
    placed = (P("tgt", "src"), P(None, None, "src"))
    return jax.shard_map(
        shards,
        mesh=mesh,
        in_specs=placed,
        out_specs=(P("src", None, "tgt"), P(None, None, "tgt", "src")),
        check_vma=False,
    )
```

```python
import functools
import math

import jax
import jax.numpy as jnp
from jax import lax
from jax.experimental import pallas as pl
from jax.experimental.pallas import tpu as pltpu
from jax.sharding import PartitionSpec as P

highest = lax.Precision.HIGHEST
MESH = pl.DeviceIdType.MESH


def nt_dot(a, b):
    return lax.dot_general(a, b, (((1,), (1,)), ((), ())), preferred_element_type=jnp.float32)


def split(value):
    high = value.astype(jnp.bfloat16)
    return high, (value - high.astype(jnp.float32)).astype(jnp.bfloat16)


def inverse_factor(a, chunk=16):
    n = a.shape[0]
    lanes = 2 * n
    m = jnp.concatenate([a, jnp.eye(n, dtype=a.dtype)], axis=1)
    blocks = [m[8 * r:8 * r + 8] for r in range(n // 8)]
    row_ids = lax.broadcasted_iota(jnp.int32, (8, lanes), 0)
    for start in range(0, n, chunk):
        cols = [{r: jnp.broadcast_to(blocks[r][:, start + q:start + q + 1], (8, lanes))
                 for r in range(start // 8, n // 8)} for q in range(chunk)]
        for q in range(chunk):
            top, inner = divmod(start + q, 8)
            inv = 1.0 / jnp.broadcast_to(cols[q][top][inner:inner + 1], (8, lanes))
            row = jnp.broadcast_to(blocks[top][inner:inner + 1], (8, lanes)) * inv
            later = {p: jnp.broadcast_to(cols[p][top][inner:inner + 1], (8, lanes)) * inv for p in range(q + 1, chunk)}
            for r in range(top, n // 8):
                mult = cols[q][r]
                if r == top:
                    mult = jnp.where(row_ids > inner, mult, 0.0)
                for p in later:
                    cols[p][r] = cols[p][r] - mult * later[p]
                blocks[r] = blocks[r] - mult * row
    m = jnp.concatenate(blocks, axis=0)
    r_ids = lax.broadcasted_iota(jnp.int32, (n, lanes), 0)
    c_ids = lax.broadcasted_iota(jnp.int32, (n, lanes), 1)
    pivots = jnp.sum(jnp.where(r_ids == c_ids, m, 0.0), axis=1, keepdims=True)
    return m[:, n:] * (1.0 / jnp.sqrt(pivots))


def mm(a, b):
    return lax.dot_general(a, b, (((1,), (0,)), ((), ())), precision=highest, preferred_element_type=jnp.float32)


def mmt(a, b):
    return lax.dot_general(a, b, (((1,), (1,)), ((), ())), precision=highest, preferred_element_type=jnp.float32)


def flip(index, mask):
    result = 0
    place = 1
    while place <= mask:
        bit = lax.rem(index // place, 2)
        result = result + place * ((1 - bit) if mask & place else bit)
        place *= 2
    return result + (index // place) * place


def remote(src, dst, send, recv, device):
    return pltpu.make_async_remote_copy(
        src_ref=src, dst_ref=dst, send_sem=send, recv_sem=recv, device_id=device, device_id_type=MESH)


class Reduction:
    def __init__(self, n, parts, pieces, summed, full, sems):
        self.n, self.parts, self.pieces, self.summed, self.full = n, parts, pieces, summed, full
        self.r_send, self.r_recv, self.g_send, self.g_recv = (sems.at[k] for k in range(4))
        self.t = lax.axis_index("tgt")

    def piece(self, d):
        to = lax.rem(self.t + d, self.n)
        return remote(self.parts.at[to], self.pieces.at[d - 1], self.r_send.at[d - 1], self.r_recv.at[d - 1], {"tgt": to})

    def share(self, d):
        to = lax.rem(self.t + d, self.n)
        return remote(self.summed, self.full.at[self.t], self.g_send.at[d - 1], self.g_recv.at[d - 1], {"tgt": to})

    def scatter(self, value):
        rows = value.shape[0] // self.n
        for p in range(self.n):
            self.parts[p] = value[p * rows:(p + 1) * rows]
        for d in range(1, self.n):
            self.piece(d).start()

    def gather(self):
        value = self.parts[self.t]
        for d in range(1, self.n):
            self.piece(d).wait_recv()
            value = value + self.pieces[d - 1]
        self.summed[...] = value
        self.full[self.t] = value
        for d in range(1, self.n):
            self.share(d).start()

    def result(self):
        for d in range(1, self.n):
            origin = lax.rem(self.t + self.n - d, self.n)
            remote(self.summed, self.full.at[origin], self.g_send.at[d - 1], self.g_recv.at[d - 1],
                   {"tgt": origin}).wait_recv()
        return jnp.concatenate([self.full[p] for p in range(self.n)], axis=0)

    def drain(self):
        for d in range(1, self.n):
            self.piece(d).wait_send()
            self.share(d).wait_send()


def moved_rows(mask, rank):
    return rank * (3 if mask % 4 == 0 else 2 if mask % 2 == 0 else 1)


def product(weights, operand):
    w_high, w_low = weights
    high, low = operand
    count = w_high.shape[0]
    both = jnp.dot(jnp.concatenate([w_high, w_low], axis=0), high, preferred_element_type=jnp.float32)
    return both[:count] + (both[count:] + jnp.dot(w_high, low, preferred_element_type=jnp.float32))


def bases_kernel(n_src, n_tgt, tiles, tile, slots, before, rank, scale,
                 kernel_hbm, probes_hbm, middle_ref, coarse_ref,
                 held, probes_ref, own, shared, stack, chip, total, moved, fits, tops, rest,
                 parts_a, pieces_a, summed_a, full_a, parts_b, pieces_b, summed_b, full_b,
                 k_sem, p_sem, a_send, a_recv, b_send, b_recv, c_send, c_recv,
                 ra_sems, rb_sems, m_send, m_recv, w_send, w_recv, hops, h_send, h_recv,
                 pivots, factors, low, pair_first, basis):
    s = lax.axis_index("src")
    t = lax.axis_index("tgt")
    core = lax.rem(s, 2)
    mate = flip(s, 1)
    across = flip(s, 2)
    half = rank // 2
    per = tiles // n_src
    first_tile = (across - lax.rem(across, 2)) * per
    first_sum = (s - lax.rem(s, 2)) * per

    def at(i):
        return lax.rem(i + first_tile, tiles)

    def sum_at(i):
        return lax.rem(i + first_sum, tiles)


    barrier = pltpu.get_barrier_semaphore()
    for mask in range(1, n_src):
        pl.semaphore_signal(barrier, inc=1, device_id={"src": flip(s, mask)}, device_id_type=MESH)
    ring = ((t + 1 - 2 * lax.rem(t, 2), t >= 0), (t - 2, t >= 2), (t + 2, t + 2 < n_tgt))
    degree = 1 + jnp.where(t >= 2, 1, 0) + jnp.where(t + 2 < n_tgt, 1, 0)

    def greet(semaphore):
        for to, exists in ring:
            @pl.when(exists)
            def _(to=to):
                pl.semaphore_signal(semaphore, inc=1, device_id={"tgt": to}, device_id_type=MESH)

    greet(barrier)

    def fetch(i):
        slot = lax.rem(i, slots)
        return pltpu.make_async_copy(
            kernel_hbm.at[pl.ds(pl.multiple_of(at(i) * tile, tile), tile)], held.at[slot], k_sem.at[slot])

    fetch_probes = pltpu.make_async_copy(probes_hbm, probes_ref, p_sem)
    fetch_probes.start()
    for i in range(min(slots, tiles)):
        fetch(i).start()

    mine = pl.multiple_of(half * core, half)
    theirs = pl.multiple_of(half * (1 - core), half)

    def share_pair(j):
        return remote(own.at[j, pl.ds(rank, rank)], shared.at[j, pl.ds(0, rank)],
                      a_send.at[0, j], a_recv.at[0, j], {"src": mate})

    def share_group(j):
        return remote(own.at[j, pl.ds(2 * rank + theirs, half)], shared.at[j, pl.ds(rank, half)],
                      a_send.at[1, j], a_recv.at[1, j], {"src": mate})

    def cross_chip(j):
        return remote(chip.at[0, j], chip.at[1, j], b_send.at[j], b_recv.at[j], {"src": across})

    def hand_over(j):
        return remote(chip.at[2, j], stack.at[j, pl.ds(2 * rank + mine, half)],
                      c_send.at[j], c_recv.at[j], {"src": mate})

    def move(mask, q):
        to = flip(s, mask)
        count = moved_rows(mask, rank)
        skip = half if (mask in (2, 3) and q == 0) else 0
        rows = pl.ds(skip, count - skip)
        return remote(stack.at[to * per + q, rows], moved.at[mask - 1, q, rows],
                      m_send.at[mask - 1, q], m_recv.at[mask - 1, q], {"src": to})

    def head(mask):
        to = flip(s, mask)
        return remote(own.at[to * per, pl.ds(0, half)], moved.at[mask - 1, 0, pl.ds(0, half)],
                      h_send.at[mask - 2], h_recv.at[mask - 2], {"src": to})

    def heads(even):
        for mask in (2, 3):
            @pl.when((lax.rem(flip(s, mask), 2) == 0) == even)
            def _(mask=mask):
                head(mask).start()

    def tell(which, ref, mask):
        return remote(ref.at[0], ref.at[mask], w_send.at[which, mask - 1], w_recv.at[which, mask - 1],
                      {"src": flip(s, mask)})

    total[...] = jnp.zeros_like(total)

    def compute(i):
        fetch(i).wait()
        own[at(i)] = nt_dot(probes_ref[...], held[lax.rem(i, slots)])

        @pl.when(i + slots < tiles)
        def _():
            fetch(i + slots).start()

    def share(i):
        share_group(at(i)).start()
        share_pair(at(i)).start()

    def send_group(i):
        j = at(i)
        share_group(j).wait_recv()
        chip[0, j] = own[j, pl.ds(2 * rank + mine, half)] + shared[j, rank:rank + half]
        cross_chip(j).start()

    def lower_gram(j):
        share_pair(j).wait_recv()
        first = own[j, 0:rank]
        second = own[j, rank:2 * rank] + shared[j, 0:rank]
        both = jnp.concatenate([first, second], axis=0)
        stack[j, 0:2 * rank] = both
        high, low = split(both)
        total[...] += nt_dot(high, jnp.concatenate([high, low], axis=0))

    def each(start, stop, *steps):
        def run(i, carry):
            for step in steps:
                step(i)
            return carry
        lax.fori_loop(start, stop, run, 0)

    rounds = n_tgt // 2 - 1

    def spread(r):
        pl.semaphore_wait(hops.at[r], degree)

        @pl.when(r + 1 < rounds)
        def _():
            greet(hops.at[r + 1])

    fetch_probes.wait()
    each(0, before, compute)
    pl.semaphore_wait(barrier, n_src - 1 + degree)
    heads(True)
    each(0, before, share)
    greet(hops.at[0])
    compute(before)
    share(before)
    each(0, before, send_group)

    def previous(step):
        return lambda i: step(i - 1)

    def spread_at(i):
        r = (i - before - 1) // 2

        @pl.when((lax.rem(i - before - 1, 2) == 0) & (r < rounds))
        def _():
            spread(r)

    each(before + 1, tiles, compute, share, previous(send_group), spread_at)
    send_group(tiles - 1)
    each(0, tiles, lower_gram)
    each(min(rounds, (tiles - before) // 2), rounds, spread)

    lower = Reduction(n_tgt, parts_a, pieces_a, summed_a, full_a, ra_sems)
    mixed = total[:, 2 * rank:]
    lower.scatter(total[:, 0:2 * rank] + (mixed + mixed.T))
    heads(False)
    late = []
    for mask in (2, 3, 1) + tuple(range(4, n_src)):
        for q in range(per):
            if mask % 4 == 0:
                late.append((mask, q))
            else:
                move(mask, q).start()

    def sum_group(i):
        j = sum_at(i)
        cross_chip(j).wait_recv()
        value = chip[0, j] + chip[1, j]
        chip[2, j] = value
        stack[j, pl.ds(2 * rank + mine, half)] = value
        hand_over(j).start()

    def upper_gram(i, carry):
        j = sum_at(i)
        hand_over(j).wait_recv()
        high, low = split(stack[j])
        top = high[2 * rank:]
        return carry + (nt_dot(top, high) + (nt_dot(top, low) + nt_dot(low[2 * rank:], high)))

    def both(j, carry):
        sum_group(j)
        return upper_gram(j - 1, carry)

    upper = Reduction(n_tgt, parts_b, pieces_b, summed_b, full_b, rb_sems)
    rows_of = lax.broadcasted_iota(jnp.int32, (rank, rank), 0)
    pivots[...] = jnp.where(rows_of == lax.broadcasted_iota(jnp.int32, (rank, rank), 1), 1.0, 0.0)

    def stage(k, carry):
        @pl.when(k == 1)
        def _():
            early = 5 * tiles // 8
            each(0, early, sum_group)
            upper_value = lax.fori_loop(0, early - 1, upper_gram, jnp.zeros((rank, 3 * rank), jnp.float32))
            lower.gather()
            upper_value = lax.fori_loop(early, tiles, both, upper_value)
            upper_value = upper_gram(tiles - 1, upper_value)
            for mask, q in late:
                move(mask, q).start()
            upper.scatter(upper_value)
            low[...] = lower.result()
            pivots[...] = low[0:rank, 0:rank]

        @pl.when(k == 2)
        def _():
            first = factors[1]
            c_pair = mmt(low[rank:, 0:rank], first)
            pivots[...] = low[rank:, rank:] - mmt(c_pair, c_pair)
            pair_first[...] = mm(c_pair, first)
            upper.gather()

        @pl.when(k == 3)
        def _():
            first, second = factors[1], factors[2]
            basis[...] = jnp.concatenate(
                [jnp.concatenate([first, jnp.zeros_like(first)], axis=1),
                 jnp.concatenate([-mm(second, pair_first[...]), second], axis=1)], axis=0)
            up_gram = upper.result()
            coef = mmt(up_gram[:, 0:2 * rank], basis[...])
            pivots[...] = up_gram[:, 2 * rank:] - mmt(coef, coef)
            fits[0] = mm(coef, basis[...])
            for mask in range(1, n_src):
                tell(0, fits, mask).start()

        factors[k] = inverse_factor(pivots[...])
        return carry

    lax.fori_loop(0, 4, stage, 0)
    tops[0] = scale * factors[3]
    for mask in range(1, n_src):
        tell(1, tops, mask).start()

    mid_weights = split(scale * basis[rank:])
    for j in range(tiles):
        middle_ref[0, :, j * tile:(j + 1) * tile] = product(mid_weights, split(stack[j, 0:2 * rank]))

    lower.drain()
    upper.drain()

    def rows(source, q, index):
        ref = moved.at[source - 1, q] if source else stack.at[s * per + q]
        return ref[index * rank:(index + 1) * rank]

    def remainder(mask):
        if mask:
            tell(0, fits, mask).wait_recv()
        fit = split(fits[mask])
        for q in range(per):
            if mask:
                move(mask, q).wait_recv()
                if mask in (2, 3) and q == 0:
                    head(mask).wait_recv()
            lower_rows = jnp.concatenate([rows(mask, q, 0), rows(mask - mask % 2, q, 1)], axis=0)
            rest[mask, q] = rows(mask - mask % 4, q, 2) - product(fit, split(lower_rows))

    def coarse_basis(mask):
        if mask:
            tell(1, tops, mask).wait_recv()
        top = split(tops[mask])
        for q in range(per):
            coarse_ref[flip(s, mask), :, 0, q * tile:(q + 1) * tile] = product(top, split(rest[mask, q]))

    for masks in ((0,), (1,), tuple(range(2, n_src))):
        for mask in masks:
            remainder(mask)
        for mask in masks:
            coarse_basis(mask)

    def finish(j):
        share_group(j).wait_send()
        share_pair(j).wait_send()
        cross_chip(j).wait_send()
        hand_over(j).wait_send()

    each(0, tiles, finish)
    for mask in range(1, n_src):
        for q in range(per):
            move(mask, q).wait_send()
        tell(0, fits, mask).wait_send()
        tell(1, tops, mask).wait_send()
    for mask in (2, 3):
        head(mask).wait_send()


def bases(kernel, probes, tile, scale):
    n_src, n_tgt = lax.axis_size("src"), lax.axis_size("tgt")
    rows, cols = kernel.shape
    total_rank = probes.shape[0]
    rank = total_rank // 3
    tiles = rows // tile
    per = tiles // n_src
    slots = min(4, tiles)
    f32 = jnp.float32
    dma = pltpu.SemaphoreType.DMA
    low, up = 2 * rank, rank
    hbm = pl.BlockSpec(memory_space=pltpu.HBM)
    vmem = pl.BlockSpec(memory_space=pltpu.VMEM)
    return pl.pallas_call(
        functools.partial(bases_kernel, n_src, n_tgt, tiles, tile, slots, min(1, tiles - 2), rank, scale),
        out_shape=(jax.ShapeDtypeStruct((1, rank, rows), f32),
                   jax.ShapeDtypeStruct((n_src, rank, 1, per * tile), f32)),
        in_specs=[hbm, hbm],
        out_specs=(vmem, vmem),
        scratch_shapes=[
            pltpu.VMEM((slots, tile, cols), kernel.dtype),
            pltpu.VMEM((total_rank, cols), probes.dtype),
            pltpu.VMEM((tiles, total_rank, tile), f32),
            pltpu.VMEM((tiles, rank + rank // 2, tile), f32),
            pltpu.VMEM((tiles, total_rank, tile), f32),
            pltpu.VMEM((3, tiles, rank // 2, tile), f32),
            pltpu.VMEM((low, 2 * low), f32),
            pltpu.VMEM((n_src - 1, per, total_rank, tile), f32),
            pltpu.VMEM((n_src, rank, low), f32), pltpu.VMEM((n_src, rank, rank), f32),
            pltpu.VMEM((n_src, per, rank, tile), f32),
            pltpu.VMEM((n_tgt, low // n_tgt, low), f32),
            pltpu.VMEM((n_tgt - 1, low // n_tgt, low), f32),
            pltpu.VMEM((low // n_tgt, low), f32),
            pltpu.VMEM((n_tgt, low // n_tgt, low), f32),
            pltpu.VMEM((n_tgt, up // n_tgt, total_rank), f32),
            pltpu.VMEM((n_tgt - 1, up // n_tgt, total_rank), f32),
            pltpu.VMEM((up // n_tgt, total_rank), f32),
            pltpu.VMEM((n_tgt, up // n_tgt, total_rank), f32),
            dma((slots,)), dma,
            dma((2, tiles)), dma((2, tiles)), dma((tiles,)), dma((tiles,)), dma((tiles,)), dma((tiles,)),
            dma((4, n_tgt - 1)), dma((4, n_tgt - 1)),
            dma((n_src - 1, per)), dma((n_src - 1, per)), dma((2, n_src - 1)), dma((2, n_src - 1)),
            pltpu.SemaphoreType.REGULAR((max(1, n_tgt // 2 - 1),)), dma((2,)), dma((2,)),
            pltpu.VMEM((rank, rank), f32), pltpu.VMEM((4, rank, rank), f32), pltpu.VMEM((low, low), f32),
            pltpu.VMEM((rank, rank), f32), pltpu.VMEM((low, low), f32),
        ],
        compiler_params=pltpu.CompilerParams(
            collective_id=0, has_side_effects=True, vmem_limit_bytes=48 * 2 ** 20),
        name="bases",
    )(kernel, pltpu.with_memory_space_constraint(probes, pltpu.HBM))


def store_kernel(middle_in, coarse_in, middle_ref, coarse_ref, sems):
    copies = [pltpu.make_async_copy(middle_in, middle_ref, sems.at[0]),
              pltpu.make_async_copy(coarse_in, coarse_ref, sems.at[1])]
    for copy in copies:
        copy.start()
    for copy in copies:
        copy.wait()


def store(middle, coarse):
    anywhere = pl.BlockSpec(memory_space=pl.ANY)
    return pl.pallas_call(
        store_kernel,
        out_shape=tuple(jax.ShapeDtypeStruct(x.shape, x.dtype) for x in (middle, coarse)),
        in_specs=[anywhere, anywhere],
        out_specs=(anywhere, anywhere),
        scratch_shapes=[pltpu.SemaphoreType.DMA((2,))],
        compiler_params=pltpu.CompilerParams(vmem_limit_bytes=2 ** 20),
        name="store",
    )(middle, coarse)


def shards(kernel, probes):
    n_src, n_tgt = lax.axis_size("src"), lax.axis_size("tgt")
    rows = kernel.shape[0]
    scale = math.sqrt(rows * n_tgt)
    levels, rank, cols = probes.shape
    tile = min(512, rows // n_src)
    return store(*bases(kernel, probes.reshape(levels * rank, cols), tile, scale))


def solution(mesh):
    placed = (P("tgt", "src"), P(None, None, "src"))
    return jax.shard_map(
        shards,
        mesh=mesh,
        in_specs=placed,
        out_specs=(P("src", None, "tgt"), P(None, None, "tgt", "src")),
        check_vma=False,
    )
```

```python
import functools
import math

import jax
import jax.numpy as jnp
from jax import lax
from jax.experimental import pallas as pl
from jax.experimental.pallas import tpu as pltpu
from jax.sharding import PartitionSpec as P

highest = lax.Precision.HIGHEST
MESH = pl.DeviceIdType.MESH


def nt_dot(a, b):
    return lax.dot_general(a, b, (((1,), (1,)), ((), ())), preferred_element_type=jnp.float32)


def split(value):
    high = value.astype(jnp.bfloat16)
    return high, (value - high.astype(jnp.float32)).astype(jnp.bfloat16)


def inverse_factor(a, chunk=16):
    n = a.shape[0]
    lanes = 2 * n
    m = jnp.concatenate([a, jnp.eye(n, dtype=a.dtype)], axis=1)
    blocks = [m[8 * r:8 * r + 8] for r in range(n // 8)]
    row_ids = lax.broadcasted_iota(jnp.int32, (8, lanes), 0)
    for start in range(0, n, chunk):
        cols = [{r: jnp.broadcast_to(blocks[r][:, start + q:start + q + 1], (8, lanes))
                 for r in range(start // 8, n // 8)} for q in range(chunk)]
        for q in range(chunk):
            top, inner = divmod(start + q, 8)
            inv = 1.0 / jnp.broadcast_to(cols[q][top][inner:inner + 1], (8, lanes))
            row = jnp.broadcast_to(blocks[top][inner:inner + 1], (8, lanes)) * inv
            later = {p: jnp.broadcast_to(cols[p][top][inner:inner + 1], (8, lanes)) * inv for p in range(q + 1, chunk)}
            for r in range(top, n // 8):
                mult = cols[q][r]
                if r == top:
                    mult = jnp.where(row_ids > inner, mult, 0.0)
                for p in later:
                    cols[p][r] = cols[p][r] - mult * later[p]
                blocks[r] = blocks[r] - mult * row
    m = jnp.concatenate(blocks, axis=0)
    r_ids = lax.broadcasted_iota(jnp.int32, (n, lanes), 0)
    c_ids = lax.broadcasted_iota(jnp.int32, (n, lanes), 1)
    pivots = jnp.sum(jnp.where(r_ids == c_ids, m, 0.0), axis=1, keepdims=True)
    return m[:, n:] * (1.0 / jnp.sqrt(pivots))


def mm(a, b):
    return lax.dot_general(a, b, (((1,), (0,)), ((), ())), precision=highest, preferred_element_type=jnp.float32)


def mmt(a, b):
    return lax.dot_general(a, b, (((1,), (1,)), ((), ())), precision=highest, preferred_element_type=jnp.float32)


def flip(index, mask):
    result = 0
    place = 1
    while place <= mask:
        bit = lax.rem(index // place, 2)
        result = result + place * ((1 - bit) if mask & place else bit)
        place *= 2
    return result + (index // place) * place


def remote(src, dst, send, recv, device):
    return pltpu.make_async_remote_copy(
        src_ref=src, dst_ref=dst, send_sem=send, recv_sem=recv, device_id=device, device_id_type=MESH)


class Reduction:
    def __init__(self, n, parts, pieces, summed, full, sems):
        self.n, self.parts, self.pieces, self.summed, self.full = n, parts, pieces, summed, full
        self.r_send, self.r_recv, self.g_send, self.g_recv = (sems.at[k] for k in range(4))
        self.t = lax.axis_index("tgt")

    def piece(self, d):
        to = lax.rem(self.t + d, self.n)
        return remote(self.parts.at[to], self.pieces.at[d - 1], self.r_send.at[d - 1], self.r_recv.at[d - 1], {"tgt": to})

    def share(self, d):
        to = lax.rem(self.t + d, self.n)
        return remote(self.summed, self.full.at[self.t], self.g_send.at[d - 1], self.g_recv.at[d - 1], {"tgt": to})

    def scatter(self, value):
        rows = value.shape[0] // self.n
        for p in range(self.n):
            self.parts[p] = value[p * rows:(p + 1) * rows]
        for d in range(1, self.n):
            self.piece(d).start()

    def gather(self):
        value = self.parts[self.t]
        for d in range(1, self.n):
            self.piece(d).wait_recv()
            value = value + self.pieces[d - 1]
        self.summed[...] = value
        self.full[self.t] = value
        for d in range(1, self.n):
            self.share(d).start()

    def result(self):
        for d in range(1, self.n):
            origin = lax.rem(self.t + self.n - d, self.n)
            remote(self.summed, self.full.at[origin], self.g_send.at[d - 1], self.g_recv.at[d - 1],
                   {"tgt": origin}).wait_recv()
        return jnp.concatenate([self.full[p] for p in range(self.n)], axis=0)

    def drain(self):
        for d in range(1, self.n):
            self.piece(d).wait_send()
            self.share(d).wait_send()


def moved_rows(mask, rank):
    return rank * (3 if mask % 4 == 0 else 2 if mask % 2 == 0 else 1)


def product(weights, operand):
    w_high, w_low = weights
    high, low = operand
    count = w_high.shape[0]
    both = jnp.dot(jnp.concatenate([w_high, w_low], axis=0), high, preferred_element_type=jnp.float32)
    return both[:count] + (both[count:] + jnp.dot(w_high, low, preferred_element_type=jnp.float32))


def bases_kernel(n_src, n_tgt, tiles, tile, slots, before, rank, scale,
                 kernel_hbm, probes_hbm, middle_ref, coarse_ref,
                 held, probes_ref, own, shared, stack, chip, total, moved, fits, tops, rest,
                 parts_a, pieces_a, summed_a, full_a, parts_b, pieces_b, summed_b, full_b,
                 k_sem, p_sem, a_send, a_recv, b_send, b_recv, c_send, c_recv,
                 ra_sems, rb_sems, m_send, m_recv, w_send, w_recv, hops, h_send, h_recv,
                 pivots, factors, low, pair_first, basis):
    s = lax.axis_index("src")
    t = lax.axis_index("tgt")
    core = lax.rem(s, 2)
    mate = flip(s, 1)
    across = flip(s, 2)
    half = rank // 2
    per = tiles // n_src
    first_tile = (across - lax.rem(across, 2)) * per
    first_sum = (s - lax.rem(s, 2)) * per

    def at(i):
        return lax.rem(i + first_tile, tiles)

    def sum_at(i):
        return lax.rem(i + first_sum, tiles)


    barrier = pltpu.get_barrier_semaphore()
    for mask in range(1, n_src):
        pl.semaphore_signal(barrier, inc=1, device_id={"src": flip(s, mask)}, device_id_type=MESH)
    ring = ((t + 1 - 2 * lax.rem(t, 2), t >= 0), (t - 2, t >= 2), (t + 2, t + 2 < n_tgt))
    degree = 1 + jnp.where(t >= 2, 1, 0) + jnp.where(t + 2 < n_tgt, 1, 0)

    def greet(semaphore):
        for to, exists in ring:
            @pl.when(exists)
            def _(to=to):
                pl.semaphore_signal(semaphore, inc=1, device_id={"tgt": to}, device_id_type=MESH)

    greet(barrier)

    def fetch(i):
        slot = lax.rem(i, slots)
        return pltpu.make_async_copy(
            kernel_hbm.at[pl.ds(pl.multiple_of(at(i) * tile, tile), tile)], held.at[slot], k_sem.at[slot])

    fetch_probes = pltpu.make_async_copy(probes_hbm, probes_ref, p_sem)
    fetch_probes.start()
    fetch(0).start()

    mine = pl.multiple_of(half * core, half)
    theirs = pl.multiple_of(half * (1 - core), half)

    def share_pair(j):
        return remote(own.at[j, pl.ds(rank, rank)], shared.at[j, pl.ds(0, rank)],
                      a_send.at[0, j], a_recv.at[0, j], {"src": mate})

    def share_group(j):
        return remote(own.at[j, pl.ds(2 * rank + theirs, half)], shared.at[j, pl.ds(rank, half)],
                      a_send.at[1, j], a_recv.at[1, j], {"src": mate})

    def cross_chip(j):
        return remote(chip.at[0, j], chip.at[1, j], b_send.at[j], b_recv.at[j], {"src": across})

    def hand_over(j):
        return remote(chip.at[2, j], stack.at[j, pl.ds(2 * rank + mine, half)],
                      c_send.at[j], c_recv.at[j], {"src": mate})

    def move(mask, q):
        to = flip(s, mask)
        count = moved_rows(mask, rank)
        skip = half if (mask in (2, 3) and q == 0) else 0
        rows = pl.ds(skip, count - skip)
        return remote(stack.at[to * per + q, rows], moved.at[mask - 1, q, rows],
                      m_send.at[mask - 1, q], m_recv.at[mask - 1, q], {"src": to})

    def head(mask):
        to = flip(s, mask)
        return remote(own.at[to * per, pl.ds(0, half)], moved.at[mask - 1, 0, pl.ds(0, half)],
                      h_send.at[mask - 2], h_recv.at[mask - 2], {"src": to})

    def heads(even):
        for mask in (2, 3):
            @pl.when((lax.rem(flip(s, mask), 2) == 0) == even)
            def _(mask=mask):
                head(mask).start()

    def tell(which, ref, mask):
        return remote(ref.at[0], ref.at[mask], w_send.at[which, mask - 1], w_recv.at[which, mask - 1],
                      {"src": flip(s, mask)})

    total[...] = jnp.zeros_like(total)

    def compute(i):
        fetch(i).wait()
        own[at(i)] = nt_dot(probes_ref[...], held[lax.rem(i, slots)])

        @pl.when(i + slots < tiles)
        def _():
            fetch(i + slots).start()

    def share(i):
        share_group(at(i)).start()
        share_pair(at(i)).start()

    def send_group(i):
        j = at(i)
        share_group(j).wait_recv()
        chip[0, j] = own[j, pl.ds(2 * rank + mine, half)] + shared[j, rank:rank + half]
        cross_chip(j).start()

    def lower_gram(j):
        share_pair(j).wait_recv()
        first = own[j, 0:rank]
        second = own[j, rank:2 * rank] + shared[j, 0:rank]
        both = jnp.concatenate([first, second], axis=0)
        stack[j, 0:2 * rank] = both
        high, low = split(both)
        total[...] += nt_dot(high, jnp.concatenate([high, low], axis=0))

    def each(start, stop, *steps):
        def run(i, carry):
            for step in steps:
                step(i)
            return carry
        lax.fori_loop(start, stop, run, 0)

    rounds = n_tgt // 2 - 1

    def spread(r):
        pl.semaphore_wait(hops.at[r], degree)

        @pl.when(r + 1 < rounds)
        def _():
            greet(hops.at[r + 1])

    fetch_probes.wait()
    for i in range(1, min(slots, tiles)):
        fetch(i).start()
    each(0, before, compute)
    pl.semaphore_wait(barrier, n_src - 1 + degree)
    heads(True)
    each(0, before, share)
    greet(hops.at[0])
    compute(before)
    share(before)
    each(0, before, send_group)

    def previous(step):
        return lambda i: step(i - 1)

    def spread_at(i):
        r = (i - before - 1) // 2

        @pl.when((lax.rem(i - before - 1, 2) == 0) & (r < rounds))
        def _():
            spread(r)

    each(before + 1, tiles, compute, share, previous(send_group), spread_at)
    send_group(tiles - 1)
    each(0, tiles, lower_gram)
    each(min(rounds, (tiles - before) // 2), rounds, spread)

    lower = Reduction(n_tgt, parts_a, pieces_a, summed_a, full_a, ra_sems)
    mixed = total[:, 2 * rank:]
    lower.scatter(total[:, 0:2 * rank] + (mixed + mixed.T))
    heads(False)
    late = []
    for mask in (2, 3, 1) + tuple(range(4, n_src)):
        for q in range(per):
            if mask % 4 == 0:
                late.append((mask, q))
            else:
                move(mask, q).start()

    def sum_group(i):
        j = sum_at(i)
        cross_chip(j).wait_recv()
        value = chip[0, j] + chip[1, j]
        chip[2, j] = value
        stack[j, pl.ds(2 * rank + mine, half)] = value
        hand_over(j).start()

    def upper_gram(i, carry):
        j = sum_at(i)
        hand_over(j).wait_recv()
        high, low = split(stack[j])
        top = high[2 * rank:]
        return carry + (nt_dot(top, high) + (nt_dot(top, low) + nt_dot(low[2 * rank:], high)))

    def both(j, carry):
        sum_group(j)
        return upper_gram(j - 1, carry)

    upper = Reduction(n_tgt, parts_b, pieces_b, summed_b, full_b, rb_sems)
    rows_of = lax.broadcasted_iota(jnp.int32, (rank, rank), 0)
    pivots[...] = jnp.where(rows_of == lax.broadcasted_iota(jnp.int32, (rank, rank), 1), 1.0, 0.0)

    def stage(k, carry):
        @pl.when(k == 1)
        def _():
            early = 5 * tiles // 8
            each(0, early, sum_group)
            upper_value = lax.fori_loop(0, early - 1, upper_gram, jnp.zeros((rank, 3 * rank), jnp.float32))
            lower.gather()
            upper_value = lax.fori_loop(early, tiles, both, upper_value)
            upper_value = upper_gram(tiles - 1, upper_value)
            for mask, q in late:
                move(mask, q).start()
            upper.scatter(upper_value)
            low[...] = lower.result()
            pivots[...] = low[0:rank, 0:rank]

        @pl.when(k == 2)
        def _():
            first = factors[1]
            c_pair = mmt(low[rank:, 0:rank], first)
            pivots[...] = low[rank:, rank:] - mmt(c_pair, c_pair)
            pair_first[...] = mm(c_pair, first)
            upper.gather()

        @pl.when(k == 3)
        def _():
            first, second = factors[1], factors[2]
            basis[...] = jnp.concatenate(
                [jnp.concatenate([first, jnp.zeros_like(first)], axis=1),
                 jnp.concatenate([-mm(second, pair_first[...]), second], axis=1)], axis=0)
            up_gram = upper.result()
            coef = mmt(up_gram[:, 0:2 * rank], basis[...])
            pivots[...] = up_gram[:, 2 * rank:] - mmt(coef, coef)
            fits[0] = mm(coef, basis[...])
            for mask in range(1, n_src):
                tell(0, fits, mask).start()

        factors[k] = inverse_factor(pivots[...])
        return carry

    lax.fori_loop(0, 4, stage, 0)
    tops[0] = scale * factors[3]
    for mask in range(1, n_src):
        tell(1, tops, mask).start()

    mid_weights = split(scale * basis[rank:])
    for j in range(tiles):
        middle_ref[0, :, j * tile:(j + 1) * tile] = product(mid_weights, split(stack[j, 0:2 * rank]))

    lower.drain()
    upper.drain()

    def rows(source, q, index):
        ref = moved.at[source - 1, q] if source else stack.at[s * per + q]
        return ref[index * rank:(index + 1) * rank]

    def remainder(mask):
        if mask:
            tell(0, fits, mask).wait_recv()
        fit = split(fits[mask])
        for q in range(per):
            if mask:
                move(mask, q).wait_recv()
                if mask in (2, 3) and q == 0:
                    head(mask).wait_recv()
            lower_rows = jnp.concatenate([rows(mask, q, 0), rows(mask - mask % 2, q, 1)], axis=0)
            rest[mask, q] = rows(mask - mask % 4, q, 2) - product(fit, split(lower_rows))

    def coarse_basis(mask):
        if mask:
            tell(1, tops, mask).wait_recv()
        top = split(tops[mask])
        for q in range(per):
            coarse_ref[flip(s, mask), :, 0, q * tile:(q + 1) * tile] = product(top, split(rest[mask, q]))

    for masks in ((0,), (1,), tuple(range(2, n_src))):
        for mask in masks:
            remainder(mask)
        for mask in masks:
            coarse_basis(mask)

    def finish(j):
        share_group(j).wait_send()
        share_pair(j).wait_send()
        cross_chip(j).wait_send()
        hand_over(j).wait_send()

    each(0, tiles, finish)
    for mask in range(1, n_src):
        for q in range(per):
            move(mask, q).wait_send()
        tell(0, fits, mask).wait_send()
        tell(1, tops, mask).wait_send()
    for mask in (2, 3):
        head(mask).wait_send()


def bases(kernel, probes, tile, scale):
    n_src, n_tgt = lax.axis_size("src"), lax.axis_size("tgt")
    rows, cols = kernel.shape
    total_rank = probes.shape[0]
    rank = total_rank // 3
    tiles = rows // tile
    per = tiles // n_src
    slots = min(4, tiles)
    f32 = jnp.float32
    dma = pltpu.SemaphoreType.DMA
    low, up = 2 * rank, rank
    hbm = pl.BlockSpec(memory_space=pltpu.HBM)
    vmem = pl.BlockSpec(memory_space=pltpu.VMEM)
    return pl.pallas_call(
        functools.partial(bases_kernel, n_src, n_tgt, tiles, tile, slots, min(1, tiles - 2), rank, scale),
        out_shape=(jax.ShapeDtypeStruct((1, rank, rows), f32),
                   jax.ShapeDtypeStruct((n_src, rank, 1, per * tile), f32)),
        in_specs=[hbm, hbm],
        out_specs=(vmem, vmem),
        scratch_shapes=[
            pltpu.VMEM((slots, tile, cols), kernel.dtype),
            pltpu.VMEM((total_rank, cols), probes.dtype),
            pltpu.VMEM((tiles, total_rank, tile), f32),
            pltpu.VMEM((tiles, rank + rank // 2, tile), f32),
            pltpu.VMEM((tiles, total_rank, tile), f32),
            pltpu.VMEM((3, tiles, rank // 2, tile), f32),
            pltpu.VMEM((low, 2 * low), f32),
            pltpu.VMEM((n_src - 1, per, total_rank, tile), f32),
            pltpu.VMEM((n_src, rank, low), f32), pltpu.VMEM((n_src, rank, rank), f32),
            pltpu.VMEM((n_src, per, rank, tile), f32),
            pltpu.VMEM((n_tgt, low // n_tgt, low), f32),
            pltpu.VMEM((n_tgt - 1, low // n_tgt, low), f32),
            pltpu.VMEM((low // n_tgt, low), f32),
            pltpu.VMEM((n_tgt, low // n_tgt, low), f32),
            pltpu.VMEM((n_tgt, up // n_tgt, total_rank), f32),
            pltpu.VMEM((n_tgt - 1, up // n_tgt, total_rank), f32),
            pltpu.VMEM((up // n_tgt, total_rank), f32),
            pltpu.VMEM((n_tgt, up // n_tgt, total_rank), f32),
            dma((slots,)), dma,
            dma((2, tiles)), dma((2, tiles)), dma((tiles,)), dma((tiles,)), dma((tiles,)), dma((tiles,)),
            dma((4, n_tgt - 1)), dma((4, n_tgt - 1)),
            dma((n_src - 1, per)), dma((n_src - 1, per)), dma((2, n_src - 1)), dma((2, n_src - 1)),
            pltpu.SemaphoreType.REGULAR((max(1, n_tgt // 2 - 1),)), dma((2,)), dma((2,)),
            pltpu.VMEM((rank, rank), f32), pltpu.VMEM((4, rank, rank), f32), pltpu.VMEM((low, low), f32),
            pltpu.VMEM((rank, rank), f32), pltpu.VMEM((low, low), f32),
        ],
        compiler_params=pltpu.CompilerParams(
            collective_id=0, has_side_effects=True, vmem_limit_bytes=48 * 2 ** 20),
        name="bases",
    )(kernel, pltpu.with_memory_space_constraint(probes, pltpu.HBM))


def store_kernel(middle_in, coarse_in, middle_ref, coarse_ref, sems):
    copies = [pltpu.make_async_copy(middle_in, middle_ref, sems.at[0]),
              pltpu.make_async_copy(coarse_in, coarse_ref, sems.at[1])]
    for copy in copies:
        copy.start()
    for copy in copies:
        copy.wait()


def store(middle, coarse):
    anywhere = pl.BlockSpec(memory_space=pl.ANY)
    return pl.pallas_call(
        store_kernel,
        out_shape=tuple(jax.ShapeDtypeStruct(x.shape, x.dtype) for x in (middle, coarse)),
        in_specs=[anywhere, anywhere],
        out_specs=(anywhere, anywhere),
        scratch_shapes=[pltpu.SemaphoreType.DMA((2,))],
        compiler_params=pltpu.CompilerParams(vmem_limit_bytes=2 ** 20),
        name="store",
    )(middle, coarse)


def shards(kernel, probes):
    n_src, n_tgt = lax.axis_size("src"), lax.axis_size("tgt")
    rows = kernel.shape[0]
    scale = math.sqrt(rows * n_tgt)
    levels, rank, cols = probes.shape
    tile = min(512, rows // n_src)
    return store(*bases(kernel, probes.reshape(levels * rank, cols), tile, scale))


def solution(mesh):
    placed = (P("tgt", "src"), P(None, None, "src"))
    return jax.shard_map(
        shards,
        mesh=mesh,
        in_specs=placed,
        out_specs=(P("src", None, "tgt"), P(None, None, "tgt", "src")),
        check_vma=False,
    )
```

```python
import functools
import math

import jax
import jax.numpy as jnp
from jax import lax
from jax.experimental import pallas as pl
from jax.experimental.pallas import tpu as pltpu
from jax.sharding import PartitionSpec as P

highest = lax.Precision.HIGHEST
MESH = pl.DeviceIdType.MESH


def nt_dot(a, b):
    return lax.dot_general(a, b, (((1,), (1,)), ((), ())), preferred_element_type=jnp.float32)


def split(value):
    high = value.astype(jnp.bfloat16)
    return high, (value - high.astype(jnp.float32)).astype(jnp.bfloat16)


def inverse_factor(a, chunk=16):
    n = a.shape[0]
    lanes = 2 * n
    m = jnp.concatenate([a, jnp.eye(n, dtype=a.dtype)], axis=1)
    blocks = [m[8 * r:8 * r + 8] for r in range(n // 8)]
    row_ids = lax.broadcasted_iota(jnp.int32, (8, lanes), 0)
    for start in range(0, n, chunk):
        cols = [{r: jnp.broadcast_to(blocks[r][:, start + q:start + q + 1], (8, lanes))
                 for r in range(start // 8, n // 8)} for q in range(chunk)]
        for q in range(chunk):
            top, inner = divmod(start + q, 8)
            inv = 1.0 / jnp.broadcast_to(cols[q][top][inner:inner + 1], (8, lanes))
            row = jnp.broadcast_to(blocks[top][inner:inner + 1], (8, lanes)) * inv
            later = {p: jnp.broadcast_to(cols[p][top][inner:inner + 1], (8, lanes)) * inv for p in range(q + 1, chunk)}
            for r in range(top, n // 8):
                mult = cols[q][r]
                if r == top:
                    mult = jnp.where(row_ids > inner, mult, 0.0)
                for p in later:
                    cols[p][r] = cols[p][r] - mult * later[p]
                blocks[r] = blocks[r] - mult * row
    m = jnp.concatenate(blocks, axis=0)
    r_ids = lax.broadcasted_iota(jnp.int32, (n, lanes), 0)
    c_ids = lax.broadcasted_iota(jnp.int32, (n, lanes), 1)
    pivots = jnp.sum(jnp.where(r_ids == c_ids, m, 0.0), axis=1, keepdims=True)
    return m[:, n:] * (1.0 / jnp.sqrt(pivots))


def mm(a, b):
    return lax.dot_general(a, b, (((1,), (0,)), ((), ())), precision=highest, preferred_element_type=jnp.float32)


def mmt(a, b):
    return lax.dot_general(a, b, (((1,), (1,)), ((), ())), precision=highest, preferred_element_type=jnp.float32)


def flip(index, mask):
    result = 0
    place = 1
    while place <= mask:
        bit = lax.rem(index // place, 2)
        result = result + place * ((1 - bit) if mask & place else bit)
        place *= 2
    return result + (index // place) * place


def remote(src, dst, send, recv, device):
    return pltpu.make_async_remote_copy(
        src_ref=src, dst_ref=dst, send_sem=send, recv_sem=recv, device_id=device, device_id_type=MESH)


class Reduction:
    def __init__(self, n, parts, pieces, summed, full, sems):
        self.n, self.parts, self.pieces, self.summed, self.full = n, parts, pieces, summed, full
        self.r_send, self.r_recv, self.g_send, self.g_recv = (sems.at[k] for k in range(4))
        self.t = lax.axis_index("tgt")

    def piece(self, d):
        to = lax.rem(self.t + d, self.n)
        return remote(self.parts.at[to], self.pieces.at[d - 1], self.r_send.at[d - 1], self.r_recv.at[d - 1], {"tgt": to})

    def share(self, d):
        to = lax.rem(self.t + d, self.n)
        return remote(self.summed, self.full.at[self.t], self.g_send.at[d - 1], self.g_recv.at[d - 1], {"tgt": to})

    def scatter(self, value):
        rows = value.shape[0] // self.n
        for p in range(self.n):
            self.parts[p] = value[p * rows:(p + 1) * rows]
        for d in range(1, self.n):
            self.piece(d).start()

    def gather(self):
        value = self.parts[self.t]
        for d in range(1, self.n):
            self.piece(d).wait_recv()
            value = value + self.pieces[d - 1]
        self.summed[...] = value
        self.full[self.t] = value
        for d in range(1, self.n):
            self.share(d).start()

    def result(self):
        for d in range(1, self.n):
            origin = lax.rem(self.t + self.n - d, self.n)
            remote(self.summed, self.full.at[origin], self.g_send.at[d - 1], self.g_recv.at[d - 1],
                   {"tgt": origin}).wait_recv()
        return jnp.concatenate([self.full[p] for p in range(self.n)], axis=0)

    def drain(self):
        for d in range(1, self.n):
            self.piece(d).wait_send()
            self.share(d).wait_send()


def moved_rows(mask, rank):
    return rank * (3 if mask % 4 == 0 else 2 if mask % 2 == 0 else 1)


def product(weights, operand):
    w_high, w_low = weights
    high, low = operand
    count = w_high.shape[0]
    both = jnp.dot(jnp.concatenate([w_high, w_low], axis=0), high, preferred_element_type=jnp.float32)
    return both[:count] + (both[count:] + jnp.dot(w_high, low, preferred_element_type=jnp.float32))


def bases_kernel(n_src, n_tgt, tiles, tile, slots, before, rank, scale,
                 kernel_hbm, probes_hbm, middle_ref, coarse_ref,
                 held, probes_ref, own, shared, stack, chip, total, moved, fits, tops, rest,
                 parts_a, pieces_a, summed_a, full_a, parts_b, pieces_b, summed_b, full_b,
                 k_sem, p_sem, a_send, a_recv, b_send, b_recv, c_send, c_recv,
                 ra_sems, rb_sems, m_send, m_recv, w_send, w_recv, hops, h_send, h_recv,
                 pivots, factors, low, pair_first, basis):
    s = lax.axis_index("src")
    t = lax.axis_index("tgt")
    core = lax.rem(s, 2)
    mate = flip(s, 1)
    across = flip(s, 2)
    half = rank // 2
    per = tiles // n_src
    first_tile = (across - lax.rem(across, 2)) * per
    first_sum = (s - lax.rem(s, 2)) * per

    def at(i):
        return lax.rem(i + first_tile, tiles)

    def sum_at(i):
        return lax.rem(i + first_sum, tiles)


    barrier = pltpu.get_barrier_semaphore()
    for mask in range(1, n_src):
        pl.semaphore_signal(barrier, inc=1, device_id={"src": flip(s, mask)}, device_id_type=MESH)
    ring = ((t + 1 - 2 * lax.rem(t, 2), t >= 0), (t - 2, t >= 2), (t + 2, t + 2 < n_tgt))
    degree = 1 + jnp.where(t >= 2, 1, 0) + jnp.where(t + 2 < n_tgt, 1, 0)

    def greet(semaphore):
        for to, exists in ring:
            @pl.when(exists)
            def _(to=to):
                pl.semaphore_signal(semaphore, inc=1, device_id={"tgt": to}, device_id_type=MESH)

    greet(barrier)

    def fetch(i):
        slot = lax.rem(i, slots)
        return pltpu.make_async_copy(
            kernel_hbm.at[pl.ds(pl.multiple_of(at(i) * tile, tile), tile)], held.at[slot], k_sem.at[slot])

    fetch_probes = pltpu.make_async_copy(probes_hbm, probes_ref, p_sem)
    fetch_probes.start()
    fetch(0).start()

    mine = pl.multiple_of(half * core, half)
    theirs = pl.multiple_of(half * (1 - core), half)

    def share_pair(j):
        return remote(own.at[j, pl.ds(rank, rank)], shared.at[j, pl.ds(0, rank)],
                      a_send.at[0, j], a_recv.at[0, j], {"src": mate})

    def share_group(j):
        return remote(own.at[j, pl.ds(2 * rank + theirs, half)], shared.at[j, pl.ds(rank, half)],
                      a_send.at[1, j], a_recv.at[1, j], {"src": mate})

    def cross_chip(j):
        return remote(chip.at[0, j], chip.at[1, j], b_send.at[j], b_recv.at[j], {"src": across})

    def hand_over(j):
        return remote(chip.at[2, j], stack.at[j, pl.ds(2 * rank + mine, half)],
                      c_send.at[j], c_recv.at[j], {"src": mate})

    def move(mask, q):
        to = flip(s, mask)
        count = moved_rows(mask, rank)
        skip = half if (mask in (2, 3) and q == 0) else 0
        rows = pl.ds(skip, count - skip)
        return remote(stack.at[to * per + q, rows], moved.at[mask - 1, q, rows],
                      m_send.at[mask - 1, q], m_recv.at[mask - 1, q], {"src": to})

    def head(mask):
        to = flip(s, mask)
        return remote(own.at[to * per, pl.ds(0, half)], moved.at[mask - 1, 0, pl.ds(0, half)],
                      h_send.at[mask - 2], h_recv.at[mask - 2], {"src": to})

    def heads(even):
        for mask in (2, 3):
            @pl.when((lax.rem(flip(s, mask), 2) == 0) == even)
            def _(mask=mask):
                head(mask).start()

    def tell(which, ref, mask):
        relayed = which == 0 and mask == 3
        return remote(ref.at[2 if relayed else 0], ref.at[mask], w_send.at[which, mask - 1],
                      w_recv.at[which, mask - 1], {"src": mate if relayed else flip(s, mask)})

    total[...] = jnp.zeros_like(total)

    def compute(i):
        fetch(i).wait()
        own[at(i)] = nt_dot(probes_ref[...], held[lax.rem(i, slots)])

        @pl.when(i + slots < tiles)
        def _():
            fetch(i + slots).start()

    def share(i):
        share_group(at(i)).start()
        share_pair(at(i)).start()

    def send_group(i):
        j = at(i)
        share_group(j).wait_recv()
        chip[0, j] = own[j, pl.ds(2 * rank + mine, half)] + shared[j, rank:rank + half]
        cross_chip(j).start()

    def lower_gram(j):
        share_pair(j).wait_recv()
        first = own[j, 0:rank]
        second = own[j, rank:2 * rank] + shared[j, 0:rank]
        both = jnp.concatenate([first, second], axis=0)
        stack[j, 0:2 * rank] = both
        high, low = split(both)
        total[...] += nt_dot(high, jnp.concatenate([high, low], axis=0))

    def each(start, stop, *steps):
        def run(i, carry):
            for step in steps:
                step(i)
            return carry
        lax.fori_loop(start, stop, run, 0)

    rounds = n_tgt // 2 - 1

    def spread(r):
        pl.semaphore_wait(hops.at[r], degree)

        @pl.when(r + 1 < rounds)
        def _():
            greet(hops.at[r + 1])

    fetch_probes.wait()
    for i in range(1, min(slots, tiles)):
        fetch(i).start()
    each(0, before, compute)
    pl.semaphore_wait(barrier, n_src - 1 + degree)
    heads(True)
    each(0, before, share)
    greet(hops.at[0])
    compute(before)
    share(before)
    each(0, before, send_group)

    def previous(step):
        return lambda i: step(i - 1)

    def spread_at(i):
        r = (i - before - 1) // 2

        @pl.when((lax.rem(i - before - 1, 2) == 0) & (r < rounds))
        def _():
            spread(r)

    each(before + 1, tiles, compute, share, previous(send_group), spread_at)
    send_group(tiles - 1)
    each(0, tiles, lower_gram)
    each(min(rounds, (tiles - before) // 2), rounds, spread)

    lower = Reduction(n_tgt, parts_a, pieces_a, summed_a, full_a, ra_sems)
    mixed = total[:, 2 * rank:]
    lower.scatter(total[:, 0:2 * rank] + (mixed + mixed.T))
    heads(False)
    late = []
    for mask in (2, 3, 1) + tuple(range(4, n_src)):
        for q in range(per):
            if mask % 4 == 0:
                late.append((mask, q))
            else:
                move(mask, q).start()

    def sum_group(i):
        j = sum_at(i)
        cross_chip(j).wait_recv()
        value = chip[0, j] + chip[1, j]
        chip[2, j] = value
        stack[j, pl.ds(2 * rank + mine, half)] = value
        hand_over(j).start()

    def upper_gram(i, carry):
        j = sum_at(i)
        hand_over(j).wait_recv()
        high, low = split(stack[j])
        top = high[2 * rank:]
        return carry + (nt_dot(top, high) + (nt_dot(top, low) + nt_dot(low[2 * rank:], high)))

    def both(j, carry):
        sum_group(j)
        return upper_gram(j - 1, carry)

    upper = Reduction(n_tgt, parts_b, pieces_b, summed_b, full_b, rb_sems)
    rows_of = lax.broadcasted_iota(jnp.int32, (rank, rank), 0)
    pivots[...] = jnp.where(rows_of == lax.broadcasted_iota(jnp.int32, (rank, rank), 1), 1.0, 0.0)

    def stage(k, carry):
        @pl.when(k == 1)
        def _():
            early = 5 * tiles // 8
            each(0, early, sum_group)
            upper_value = lax.fori_loop(0, early - 1, upper_gram, jnp.zeros((rank, 3 * rank), jnp.float32))
            lower.gather()
            upper_value = lax.fori_loop(early, tiles, both, upper_value)
            upper_value = upper_gram(tiles - 1, upper_value)
            for mask, q in late:
                move(mask, q).start()
            upper.scatter(upper_value)
            low[...] = lower.result()
            pivots[...] = low[0:rank, 0:rank]

        @pl.when(k == 2)
        def _():
            first = factors[1]
            c_pair = mmt(low[rank:, 0:rank], first)
            pivots[...] = low[rank:, rank:] - mmt(c_pair, c_pair)
            pair_first[...] = mm(c_pair, first)
            upper.gather()

        @pl.when(k == 3)
        def _():
            first, second = factors[1], factors[2]
            basis[...] = jnp.concatenate(
                [jnp.concatenate([first, jnp.zeros_like(first)], axis=1),
                 jnp.concatenate([-mm(second, pair_first[...]), second], axis=1)], axis=0)
            up_gram = upper.result()
            coef = mmt(up_gram[:, 0:2 * rank], basis[...])
            pivots[...] = up_gram[:, 2 * rank:] - mmt(coef, coef)
            fits[0] = mm(coef, basis[...])
            for mask in range(1, n_src):
                if mask != 3:
                    tell(0, fits, mask).start()

        factors[k] = inverse_factor(pivots[...])
        return carry

    lax.fori_loop(0, 4, stage, 0)
    tops[0] = scale * factors[3]
    for mask in range(1, n_src):
        tell(1, tops, mask).start()

    mid_weights = split(scale * basis[rank:])
    for j in range(tiles):
        middle_ref[0, :, j * tile:(j + 1) * tile] = product(mid_weights, split(stack[j, 0:2 * rank]))

    lower.drain()
    upper.drain()

    def rows(source, q, index):
        ref = moved.at[source - 1, q] if source else stack.at[s * per + q]
        return ref[index * rank:(index + 1) * rank]

    def remainder(mask):
        if mask:
            tell(0, fits, mask).wait_recv()
        if mask == 2:
            tell(0, fits, 3).start()
        fit = split(fits[mask])
        for q in range(per):
            if mask:
                move(mask, q).wait_recv()
                if mask in (2, 3) and q == 0:
                    head(mask).wait_recv()
            lower_rows = jnp.concatenate([rows(mask, q, 0), rows(mask - mask % 2, q, 1)], axis=0)
            rest[mask, q] = rows(mask - mask % 4, q, 2) - product(fit, split(lower_rows))

    def coarse_basis(mask):
        if mask:
            tell(1, tops, mask).wait_recv()
        top = split(tops[mask])
        for q in range(per):
            coarse_ref[flip(s, mask), :, 0, q * tile:(q + 1) * tile] = product(top, split(rest[mask, q]))

    for masks in ((0,), (1,), tuple(range(2, n_src))):
        for mask in masks:
            remainder(mask)
        for mask in masks:
            coarse_basis(mask)

    def finish(j):
        share_group(j).wait_send()
        share_pair(j).wait_send()
        cross_chip(j).wait_send()
        hand_over(j).wait_send()

    each(0, tiles, finish)
    for mask in range(1, n_src):
        for q in range(per):
            move(mask, q).wait_send()
        tell(0, fits, mask).wait_send()
        tell(1, tops, mask).wait_send()
    for mask in (2, 3):
        head(mask).wait_send()


def bases(kernel, probes, tile, scale):
    n_src, n_tgt = lax.axis_size("src"), lax.axis_size("tgt")
    rows, cols = kernel.shape
    total_rank = probes.shape[0]
    rank = total_rank // 3
    tiles = rows // tile
    per = tiles // n_src
    slots = min(4, tiles)
    f32 = jnp.float32
    dma = pltpu.SemaphoreType.DMA
    low, up = 2 * rank, rank
    hbm = pl.BlockSpec(memory_space=pltpu.HBM)
    vmem = pl.BlockSpec(memory_space=pltpu.VMEM)
    return pl.pallas_call(
        functools.partial(bases_kernel, n_src, n_tgt, tiles, tile, slots, min(1, tiles - 2), rank, scale),
        out_shape=(jax.ShapeDtypeStruct((1, rank, rows), f32),
                   jax.ShapeDtypeStruct((n_src, rank, 1, per * tile), f32)),
        in_specs=[hbm, hbm],
        out_specs=(vmem, vmem),
        scratch_shapes=[
            pltpu.VMEM((slots, tile, cols), kernel.dtype),
            pltpu.VMEM((total_rank, cols), probes.dtype),
            pltpu.VMEM((tiles, total_rank, tile), f32),
            pltpu.VMEM((tiles, rank + rank // 2, tile), f32),
            pltpu.VMEM((tiles, total_rank, tile), f32),
            pltpu.VMEM((3, tiles, rank // 2, tile), f32),
            pltpu.VMEM((low, 2 * low), f32),
            pltpu.VMEM((n_src - 1, per, total_rank, tile), f32),
            pltpu.VMEM((n_src, rank, low), f32), pltpu.VMEM((n_src, rank, rank), f32),
            pltpu.VMEM((n_src, per, rank, tile), f32),
            pltpu.VMEM((n_tgt, low // n_tgt, low), f32),
            pltpu.VMEM((n_tgt - 1, low // n_tgt, low), f32),
            pltpu.VMEM((low // n_tgt, low), f32),
            pltpu.VMEM((n_tgt, low // n_tgt, low), f32),
            pltpu.VMEM((n_tgt, up // n_tgt, total_rank), f32),
            pltpu.VMEM((n_tgt - 1, up // n_tgt, total_rank), f32),
            pltpu.VMEM((up // n_tgt, total_rank), f32),
            pltpu.VMEM((n_tgt, up // n_tgt, total_rank), f32),
            dma((slots,)), dma,
            dma((2, tiles)), dma((2, tiles)), dma((tiles,)), dma((tiles,)), dma((tiles,)), dma((tiles,)),
            dma((4, n_tgt - 1)), dma((4, n_tgt - 1)),
            dma((n_src - 1, per)), dma((n_src - 1, per)), dma((2, n_src - 1)), dma((2, n_src - 1)),
            pltpu.SemaphoreType.REGULAR((max(1, n_tgt // 2 - 1),)), dma((2,)), dma((2,)),
            pltpu.VMEM((rank, rank), f32), pltpu.VMEM((4, rank, rank), f32), pltpu.VMEM((low, low), f32),
            pltpu.VMEM((rank, rank), f32), pltpu.VMEM((low, low), f32),
        ],
        compiler_params=pltpu.CompilerParams(
            collective_id=0, has_side_effects=True, vmem_limit_bytes=48 * 2 ** 20),
        name="bases",
    )(kernel, pltpu.with_memory_space_constraint(probes, pltpu.HBM))


def store_kernel(middle_in, coarse_in, middle_ref, coarse_ref, sems):
    copies = [pltpu.make_async_copy(middle_in, middle_ref, sems.at[0]),
              pltpu.make_async_copy(coarse_in, coarse_ref, sems.at[1])]
    for copy in copies:
        copy.start()
    for copy in copies:
        copy.wait()


def store(middle, coarse):
    anywhere = pl.BlockSpec(memory_space=pl.ANY)
    return pl.pallas_call(
        store_kernel,
        out_shape=tuple(jax.ShapeDtypeStruct(x.shape, x.dtype) for x in (middle, coarse)),
        in_specs=[anywhere, anywhere],
        out_specs=(anywhere, anywhere),
        scratch_shapes=[pltpu.SemaphoreType.DMA((2,))],
        compiler_params=pltpu.CompilerParams(vmem_limit_bytes=2 ** 20),
        name="store",
    )(middle, coarse)


def shards(kernel, probes):
    n_src, n_tgt = lax.axis_size("src"), lax.axis_size("tgt")
    rows = kernel.shape[0]
    scale = math.sqrt(rows * n_tgt)
    levels, rank, cols = probes.shape
    tile = min(512, rows // n_src)
    return store(*bases(kernel, probes.reshape(levels * rank, cols), tile, scale))


def solution(mesh):
    placed = (P("tgt", "src"), P(None, None, "src"))
    return jax.shard_map(
        shards,
        mesh=mesh,
        in_specs=placed,
        out_specs=(P("src", None, "tgt"), P(None, None, "tgt", "src")),
        check_vma=False,
    )
```
